32 devices in a mesh: wheel: 16 (over z, x, core), slab: 2 (over y).
Axes of the slice: x: 2, y: 2, z: 4, core: 2. Of those that a mesh axis runs over, the one named last changes fastest.
Arguments:
- krylov_block: float32 [2, 32, 3, 16, 512], P(None, 'wheel', None, None, 'slab'), may hold values from -6 to 6
- blade_class: int32 [32], P('wheel'), may hold values from 0 to 3
- neighbors: int32 [8, 512], P(None, 'slab'), may hold values from 0 to 511
- iface_rows: int32 [2, 128], P(None, 'slab'), may hold values from 0 to 255
- face_rows: int32 [2, 128], P(None, 'slab'), may hold values from 0 to 255
- stiffness: float32 [3, 3, 8, 512], P(None, None, None, 'slab'), may hold values from -1.25 to 1.25
- lumped_mass: float32 [3, 512], P(None, 'slab'), may hold values from 0.5 to 2
- precond: bfloat16 [16, 16, 384, 384], P('wheel', 'slab'), may hold values from -0.3125 to 0.3125
Outputs:
- preconditioned: float32 [16, 16, 16, 384], P('wheel', 'slab')
The draws below stay inside these ranges and needn't reach their ends.
Inputs may be any that keep to these rules, and one draw needn't show every extreme that they name: `neighbors`: extended numbering: own nodes first (256), then 64 from the lower slab, 64 from the upper slab, 64 from the previous sector, 64 from the next sector.
All inputs are finite; a program needn't handle non-finite values.
Results may differ from the reference program's by a relative error of at most 0.0039.
Values may be sent and summed in bfloat16 or wider, within the bound.
No kernel may reach another device: no remote copies, remote signals or barrier semaphores. Data moves between devices by JAX's collectives and lax.ppermute only.
A program may use at most 64 MiB of HBM per device.

```python
import math
import jax
import jax.numpy as jnp
from jax import lax

NODES_DEV = 256
VECS = 16
NB = 8
IFACE = 64
CYC = 64
GROUP = 32
SECTORS = 32
PAIRS = 16
NODES = 512
GROUPS = 16
BLOCK = 384
N_SLAB = 2


def set_ends(drawn, key, smallest, high):
    extent = drawn.shape
    spot = [jax.random.randint(jax.random.fold_in(key, axis), (), 0, extent[axis]) for axis in range(len(extent))]
    drawn = drawn.at[tuple(spot)].set(smallest)
    longest = extent.index(max(extent))
    spot[longest] = (spot[longest] + 1) % extent[longest]
    return drawn.at[tuple(spot)].set(high)


def level_of(rng, extent, cuts, least, high):
    factor_of = 1.0
    for position, parts in cuts:
        steps = jax.random.uniform(jax.random.fold_in(jax.random.fold_in(rng, 6), position), (parts,), jnp.float32, least / len(cuts), high / len(cuts))
        factor_of = factor_of * jnp.repeat(jnp.exp(steps), extent[position] // parts).reshape((-1,) + (1,) * (len(extent) - 1 - position))
    return factor_of


def scatter_about(key, extent, width, most, split=(), held_as=jnp.bfloat16):
    level = level_of(key, extent, split, -0.22, 0.18) if split else 1.0
    drawn = jax.random.normal(key, extent, jnp.float32) * width * level
    return jnp.minimum(jnp.maximum(drawn, -most), most).astype(held_as)


def setup_inputs(seed: int = 0) -> dict:
    seeds = jax.random.split(jax.random.key(seed), 9)
    return {
        "krylov_block": scatter_about(seeds[0], (2, SECTORS, 3, VECS, NODES), 1.0, 6.0, ((1, 16), (4, 2)), jnp.float32),
        "blade_class": set_ends(jax.random.randint(seeds[1], (SECTORS,), 0, 4), jax.random.fold_in(seeds[1], 1), 0, 3).astype(jnp.int32),
        "neighbors": set_ends(jax.random.randint(seeds[2], (NB, NODES), 0, NODES_DEV + 2 * IFACE + 2 * CYC), jax.random.fold_in(seeds[2], 1), 0, (NODES_DEV + 2 * IFACE + 2 * CYC) - 1).astype(jnp.int32),
        "iface_rows": set_ends(jax.random.randint(seeds[3], (2, IFACE * N_SLAB), 0, NODES_DEV), jax.random.fold_in(seeds[3], 1), 0, NODES_DEV - 1).astype(jnp.int32),
        "face_rows": set_ends(jax.random.randint(seeds[4], (2, CYC * N_SLAB), 0, NODES_DEV), jax.random.fold_in(seeds[4], 1), 0, NODES_DEV - 1).astype(jnp.int32),
        "stiffness": scatter_about(seeds[5], (3, 3, NB, NODES), (3 * NB) ** -0.5, 1.25, ((3, 2),), jnp.float32),
        "lumped_mass": jnp.clip(jnp.exp(math.log(2.0) - 1.3862944 * jax.random.uniform(seeds[6], (3, NODES), jnp.float32) ** level_of(seeds[6], (3, NODES), ((1, 2),), -0.2, 0.2)), 0.5, 2.0),
        "precond": scatter_about(seeds[7], (PAIRS, GROUPS, BLOCK, BLOCK), BLOCK ** -0.5, 0.3125, ((0, 16), (1, 2))),
    }


damping_ratio = 0.5
gyro_rate = 0.8
shift_value = 0.3
class_step = 0.125

def basis(row_ids, col_ids, sectors_all):
    pair_id = row_ids[:, None] // 2
    part_id = row_ids[:, None] % 2
    sector_id = col_ids[None, :]
    phases = pair_id * sector_id % sectors_all
    angles = 2.0 * math.pi / sectors_all * phases.astype(jnp.float32)
    parity = (1 - 2 * (sector_id % 2)).astype(jnp.float32)
    edge_rows = jnp.where(part_id == 0, jnp.ones_like(angles), parity * jnp.ones_like(angles)) * math.sqrt(1.0 / sectors_all)
    inner_rows = jnp.where(part_id == 0, jnp.cos(angles), jnp.sin(angles)) * math.sqrt(2.0 / sectors_all)
    return jnp.where(pair_id == 0, edge_rows, inner_rows).astype(jnp.float32)

def arrange(harmonic):
    pair_rows, states, comps, vectors, nodes = harmonic.shape
    shaped = harmonic.reshape(pair_rows // 2, 2, states, comps, vectors, nodes // GROUP, GROUP)
    shaped = shaped.transpose(0, 5, 4, 1, 2, 3, 6)
    return shaped.reshape(pair_rows // 2, nodes // GROUP, vectors, 4 * comps * GROUP)

def reference(krylov_block, blade_class, neighbors, iface_rows, face_rows, stiffness, lumped_mass, precond):
    displacement = krylov_block[0]
    velocity = krylov_block[1]
    moved_field = displacement + damping_ratio * velocity
    rim_width = iface_rows.shape[1] // N_SLAB
    face_width = face_rows.shape[1] // N_SLAB
    pieces = []
    for slab_index in range(N_SLAB):
        first_node = slab_index * NODES_DEV
        own_nodes = moved_field[..., first_node:first_node + NODES_DEV]
        if slab_index > 0:
            below_nodes = moved_field[..., first_node - NODES_DEV:first_node]
            from_lower = jnp.take(below_nodes, iface_rows[1, (slab_index - 1) * rim_width:slab_index * rim_width], axis=3)
        else:
            from_lower = jnp.zeros(own_nodes.shape[:3] + (rim_width,), jnp.float32)
        if slab_index < N_SLAB - 1:
            above_nodes = moved_field[..., first_node + NODES_DEV:first_node + 2 * NODES_DEV]
            from_upper = jnp.take(above_nodes, iface_rows[0, (slab_index + 1) * rim_width:(slab_index + 2) * rim_width], axis=3)
        else:
            from_upper = jnp.zeros(own_nodes.shape[:3] + (rim_width,), jnp.float32)
        left_face = jnp.take(own_nodes, face_rows[0, slab_index * face_width:(slab_index + 1) * face_width], axis=3)
        right_face = jnp.take(own_nodes, face_rows[1, slab_index * face_width:(slab_index + 1) * face_width], axis=3)
        from_prev = jnp.roll(right_face, 1, axis=0)
        from_next = jnp.roll(left_face, -1, axis=0)
        extended = jnp.concatenate((own_nodes, from_lower, from_upper, from_prev, from_next), axis=3)
        picked = jnp.take(extended, neighbors[:, first_node:first_node + NODES_DEV], axis=3)
        pieces.append(jnp.einsum('cdkn,sdvkn->scvn', stiffness[..., first_node:first_node + NODES_DEV], picked, precision=lax.Precision.HIGHEST))
    restore = jnp.concatenate(pieces, axis=3)
    scale = (1.0 + class_step * blade_class.astype(jnp.float32))[:, None, None, None]
    gyro = gyro_rate * jnp.stack((-lumped_mass[0] * velocity[:, 1], lumped_mass[1] * velocity[:, 0], jnp.zeros_like(velocity[:, 2])), axis=1)
    res_disp = velocity - shift_value * displacement
    res_velo = -scale * restore - gyro - shift_value * lumped_mass[None, :, None, :] * velocity
    residual = jnp.stack((res_disp, res_velo), axis=0)
    sectors_all = residual.shape[1]
    table = basis(jnp.arange(sectors_all, dtype=jnp.int32), jnp.arange(sectors_all, dtype=jnp.int32), sectors_all)
    harmonic = jnp.einsum('bs,tscvn->btcvn', table, residual, precision=lax.Precision.HIGHEST).astype(jnp.bfloat16)
    lhs = arrange(harmonic)
    return jnp.einsum('pgvj,pgij->pgvi', lhs.astype(jnp.float32), precond.astype(jnp.float32))
```

```python
import functools
import math

import jax
import jax.numpy as jnp
import numpy as np
from jax import lax
from jax.experimental import pallas as pl
from jax.experimental.pallas import tpu as pltpu
from jax.sharding import PartitionSpec as P

GROUP = 32
LANES = 128
COMPS = 3

damping_ratio = 0.5
gyro_rate = 0.8
shift_value = 0.3
class_step = 0.125

BF = jnp.bfloat16
F32 = jnp.float32


def basis(sectors_all):
    row = np.arange(sectors_all)[:, None]
    sector = np.arange(sectors_all)[None, :]
    pair, part = row // 2, row % 2
    angles = 2.0 * math.pi / sectors_all * (pair * sector % sectors_all)
    edge = np.where(part == 0, 1.0, 1.0 - 2.0 * (sector % 2)) * math.sqrt(1.0 / sectors_all)
    inner = np.where(part == 0, np.cos(angles), np.sin(angles)) * math.sqrt(2.0 / sectors_all)
    return np.where(pair == 0, edge, inner)


def selection(wheel, local, rows, fields):
    sectors = wheel * local
    out = np.zeros((len(fields), COMPS, sectors, wheel, rows), np.float32)
    for f, weights in enumerate(fields):
        for t, weight in enumerate(weights):
            for c in range(COMPS):
                for s in range(sectors):
                    out[f, c, s, s // local, (t * local + s % local) * COMPS + c] = weight
    return out.reshape(len(fields) * COMPS * sectors, wheel * rows)


def scale_selection(wheel, local, rows):
    sectors = wheel * local
    out = np.zeros((sectors, wheel, rows), np.float32)
    for s in range(sectors):
        out[s, s // local, 2 * local * COMPS + s % local] = 1.0
    return out.reshape(sectors, wheel * rows)


def transform(sectors):
    table = basis(sectors).reshape(sectors // 2, 2, sectors)
    out = np.zeros((2, 2, COMPS, sectors // 2, 2, COMPS, sectors), np.float32)
    for t in range(2):
        for c in range(COMPS):
            out[:, t, c, :, t, c, :] = table.transpose(1, 0, 2)
    return out.reshape(2 * 2 * COMPS * (sectors // 2), 2 * COMPS * sectors)


def split(x):
    high = x.astype(BF)
    return high, (x - high.astype(F32)).astype(BF)


def dot(a, b):
    return jnp.dot(a, b, preferred_element_type=F32)


def pack_body(vecs, local, copies, krylov, blade, iface, out, rows, sems):
    halves = rows.shape[0]
    data = krylov.shape[0]
    moves = [
        pltpu.make_async_copy(
            krylov.at[:, pl.ds(h * LANES, LANES)], rows.at[h, pl.ds(0, data)], sems.at[h]
        )
        for h in range(halves)
    ]
    for move in moves:
        move.start()
    width = iface.shape[1]
    for h in range(halves):
        at = data
        for l in range(local):
            scale = 1.0 + class_step * blade[l].astype(F32)
            rows[h, at : at + vecs, :] = jnp.full((vecs, LANES), scale, F32)
            at += vecs
        for side in range(2):
            rows[h, at : at + vecs, :] = jnp.zeros((vecs, LANES), F32)
            if h == 0:
                rows[h, at : at + vecs, 0:width] = jnp.broadcast_to(
                    iface[side : side + 1, :].astype(F32), (vecs, width)
                )
            at += vecs
    for h, move in enumerate(moves):
        move.wait()
        for v in range(vecs):
            chunk = rows[h, pl.ds(v, rows.shape[1] // vecs, stride=vecs), :].astype(BF)
            for i in range(copies):
                out[v * copies + i, :, h * LANES : (h + 1) * LANES] = chunk


def tables_body(neighbors, faces, onehot, pick):
    count, nodes = neighbors.shape
    extended = onehot.shape[0]
    index = lax.broadcasted_iota(jnp.int32, (extended, nodes), 0)
    for k in range(count):
        hit = index == neighbors[k : k + 1, :]
        onehot[:, k * nodes : (k + 1) * nodes] = jnp.where(hit, 1.0, 0.0).astype(BF)
    width = faces.shape[1]
    index = lax.broadcasted_iota(jnp.int32, (nodes, width), 0)
    for i, side in enumerate((1, 0)):
        hit = index == faces[side : side + 1, :]
        pick[:, i * width : (i + 1) * width] = jnp.where(hit, 1.0, 0.0).astype(BF)


def residual_body(
    slabs, wheel, local, width, x, *refs
):
    lows = refs[: len(refs) - 11]
    onehot, pick, stiffness, mass, sel, sel_scale, sel_moved, table, out, rim, rows = refs[-11:]
    nodes = x.shape[-1]
    sectors = wheel * local
    count = stiffness.shape[2]
    slab = lax.axis_index("slab")
    height = x.shape[-2]
    extras = 2 * local * COMPS + local
    if slabs == 2:
        own = x[:, pl.ds(slab, 1)].reshape(wheel * height, nodes)
        sides = (x[:, pl.ds(1 - slab, 1)].reshape(wheel * height, nodes),)
    else:
        own = x[...].reshape(wheel * height, nodes)
        sides = tuple(ref[...].reshape(wheel * height, nodes) for ref in lows)

    uv = dot(sel[...], own)
    block = COMPS * sectors
    u, v = uv[:block], uv[block : 2 * block]
    scale = dot(sel_scale[...], own)
    moved = jnp.concatenate(split(u + damping_ratio * v), axis=0)

    index = lax.broadcasted_iota(jnp.int32, (nodes, width), 0)
    for i in range(2):
        side = sides[i % len(sides)]
        row = extras + 1 - i
        names = side[row : row + 1, 0:width].astype(F32).astype(jnp.int32)
        valid = (slab > 0) if i == 0 else (slab < slabs - 1)
        hit = (index == names) & valid
        rim[:, i * width : (i + 1) * width] = jnp.where(hit, 1.0, 0.0).astype(BF)
    if len(sides) == 1:
        other = jnp.concatenate(split(dot(sel_moved[...], sides[0])), axis=0)
        rims = dot(other, rim[...])
    else:
        parts = [
            dot(jnp.concatenate(split(dot(sel_moved[...], side)), axis=0), rim[...])
            for side in sides
        ]
        lane = lax.broadcasted_iota(jnp.int32, parts[0].shape, 1)
        rims = jnp.where(lane < width, parts[0], parts[1])

    faces = dot(moved, pick[...])
    turned = []
    for i in range(2 * COMPS):
        part = faces[i * sectors : (i + 1) * sectors]
        lane = lax.broadcasted_iota(jnp.int32, part.shape, 1)
        before = pltpu.roll(part, 1, axis=0)
        after = pltpu.roll(part, sectors - 1, axis=0)
        turned.append(jnp.where(lane < width, before, after))
    extended = jnp.concatenate(
        (moved, rims.astype(BF), jnp.concatenate(turned, axis=0).astype(BF)), axis=1
    )

    restore = [None] * COMPS
    for k in range(count):
        picked = dot(extended, onehot[:, k * nodes : (k + 1) * nodes])
        picked = picked[:block] + picked[block:]
        for d in range(COMPS):
            term = picked[d * sectors : (d + 1) * sectors]
            for c in range(COMPS):
                part = stiffness[c, d, k : k + 1, :] * term
                restore[c] = part if restore[c] is None else restore[c] + part

    vc = [v[c * sectors : (c + 1) * sectors] for c in range(COMPS)]
    lumped = [mass[c : c + 1, :] for c in range(COMPS)]
    gyro = (-(gyro_rate * lumped[0]) * vc[1], (gyro_rate * lumped[1]) * vc[0], None)
    residual = [v - shift_value * u]
    for c in range(COMPS):
        part = -scale * restore[c] - (shift_value * lumped[c]) * vc[c]
        residual.append(part if gyro[c] is None else part - gyro[c])
    high, low = split(jnp.concatenate(residual, axis=0))
    harmonic = dot(table[...], jnp.concatenate((high, low, high), axis=0))
    halves = nodes // LANES
    kinds = 4 * COMPS
    pairs = sectors // 2
    for h in range(halves):
        for r in range(kinds):
            rows[pl.ds(h * kinds + r, pairs, stride=halves * kinds), :] = harmonic[
                r * pairs : (r + 1) * pairs, h * LANES : (h + 1) * LANES
            ]
    out[...] = rows[...].astype(BF).reshape(out.shape)


def apply_body(vecs, spread, y, precond, out, rows):
    kinds = 4 * COMPS
    per = LANES // GROUP
    chunk = y.shape[1]
    halves = chunk // kinds
    rows[...] = y[...].astype(F32).reshape(rows.shape)
    lane = lax.broadcasted_iota(jnp.int32, (vecs, LANES), 1)
    for h in range(halves):
        tiles = [[] for _ in range(per)]
        for j in range(kinds // per):
            blocks = [
                rows[pl.ds(h * kinds + j * per + r, vecs, stride=chunk * spread), :]
                for r in range(per)
            ]
            step = per // 2
            while step:
                shift = step * GROUP
                upper = (lane // shift) % 2 == 1
                fresh = list(blocks)
                for r in range(per):
                    if r & step == 0:
                        a, b = blocks[r], blocks[r + step]
                        fresh[r] = jnp.where(upper, pltpu.roll(b, shift, axis=1), a)
                        fresh[r + step] = jnp.where(
                            upper, b, pltpu.roll(a, LANES - shift, axis=1)
                        )
                blocks = fresh
                step //= 2
            for g in range(per):
                tiles[g].append(blocks[g].astype(BF))
        for g in range(per):
            lhs = jnp.concatenate(tiles[g], axis=1)
            out[h * per + g] = lax.dot_general(
                lhs,
                precond[h * per + g],
                (((1,), (1,)), ((), ())),
                preferred_element_type=F32,
            )


def on_device(
    wheel, slabs, krylov_block, blade_class, neighbors, iface_rows, face_rows, stiffness, lumped_mass, precond
):
    states, local, comps, vecs, nodes = krylov_block.shape
    width = iface_rows.shape[1]
    spread = wheel // vecs
    sectors = wheel * local
    height = 2 * local * comps + local + 2
    count = neighbors.shape[0]
    extended = nodes + 4 * width
    vmem = pl.BlockSpec(memory_space=pltpu.VMEM)
    smem = pl.BlockSpec(memory_space=pltpu.SMEM)
    anywhere = pl.BlockSpec(memory_space=pl.ANY)

    fan = slabs if slabs == 2 else 1
    packed = pl.pallas_call(
        functools.partial(pack_body, vecs, local, spread * fan),
        out_shape=jax.ShapeDtypeStruct((wheel * fan, height, nodes), BF),
        in_specs=[anywhere, smem, vmem],
        out_specs=vmem,
        scratch_shapes=[
            pltpu.VMEM((nodes // LANES, height * vecs, LANES), F32),
            pltpu.SemaphoreType.DMA((nodes // LANES,)),
        ],
    )(krylov_block.reshape(states * local * comps * vecs, nodes), blade_class, iface_rows)
    onehot, pick = pl.pallas_call(
        tables_body,
        out_shape=(
            jax.ShapeDtypeStruct((extended, count * nodes), BF),
            jax.ShapeDtypeStruct((nodes, 2 * width), BF),
        ),
        in_specs=[vmem, vmem],
        out_specs=(vmem, vmem),
    )(neighbors, face_rows)
    if slabs == 2:
        got = lax.all_to_all(packed, ("wheel", "slab"), 0, 0, tiled=True)
        got = got.reshape(wheel, slabs, height, nodes)
        sides = ()
    else:
        got = lax.all_to_all(packed, "wheel", 0, 0, tiled=True)
        up = [(i, i + 1) for i in range(slabs - 1)]
        down = [(i + 1, i) for i in range(slabs - 1)]
        sides = (lax.ppermute(got, "slab", up), lax.ppermute(got, "slab", down))

    sel = selection(wheel, local, height, ((1.0, 0.0), (0.0, 1.0)))
    sel_moved = selection(wheel, local, height, ((1.0, damping_ratio),))
    sel_scale = scale_selection(wheel, local, height)
    table = transform(sectors)
    high = table.astype(jnp.bfloat16)
    low = (table - high.astype(np.float32)).astype(jnp.bfloat16)
    table = np.concatenate((high, high, low), axis=1)
    kinds = 4 * comps
    pairs = sectors // 2
    chunk = kinds * (nodes // LANES)
    sent = pl.pallas_call(
        functools.partial(residual_body, slabs, wheel, local, width),
        out_shape=jax.ShapeDtypeStruct((pairs, chunk, LANES), BF),
        in_specs=[vmem] * (9 + len(sides)),
        out_specs=vmem,
        scratch_shapes=[
            pltpu.VMEM((nodes, 2 * width), BF),
            pltpu.VMEM((pairs * chunk, LANES), F32),
        ],
    )(
        got,
        *sides,
        onehot,
        pick,
        stiffness,
        lumped_mass,
        jnp.asarray(sel, BF),
        jnp.asarray(sel_scale, BF),
        jnp.asarray(sel_moved, BF),
        jnp.asarray(table),
    )
    back = lax.all_to_all(sent, "wheel", 0, 0, tiled=True)
    owned, groups, order, _ = precond.shape
    out = pl.pallas_call(
        functools.partial(apply_body, vecs, spread),
        out_shape=jax.ShapeDtypeStruct((groups, vecs, order), F32),
        in_specs=[vmem, vmem],
        out_specs=vmem,
        scratch_shapes=[pltpu.VMEM((wheel * chunk, LANES), F32)],
    )(back, precond.reshape(groups, order, order))
    return out.reshape(owned, groups, vecs, order)


def solution(mesh):
    return jax.shard_map(
        functools.partial(on_device, mesh.shape["wheel"], mesh.shape["slab"]),
        mesh=mesh,
        in_specs=(
            P(None, "wheel", None, None, "slab"),
            P("wheel"),
            P(None, "slab"),
            P(None, "slab"),
            P(None, "slab"),
            P(None, None, None, "slab"),
            P(None, "slab"),
            P("wheel", "slab", None, None),
        ),
        out_specs=P("wheel", "slab", None, None),
        check_vma=False,
    )
```

```python
import functools
import math

import jax
import jax.numpy as jnp
import numpy as np
from jax import lax
from jax.experimental import pallas as pl
from jax.experimental.pallas import tpu as pltpu
from jax.sharding import PartitionSpec as P

GROUP = 32
LANES = 128
COMPS = 3

damping_ratio = 0.5
gyro_rate = 0.8
shift_value = 0.3
class_step = 0.125

BF = jnp.bfloat16
F32 = jnp.float32
LIMIT = 16 << 20


def hold(x):
    return pltpu.with_memory_space_constraint(x, pltpu.HBM)


def near(x):
    return pltpu.with_memory_space_constraint(x, pltpu.VMEM)


def basis(sectors_all):
    row = np.arange(sectors_all)[:, None]
    sector = np.arange(sectors_all)[None, :]
    pair, part = row // 2, row % 2
    angles = 2.0 * math.pi / sectors_all * (pair * sector % sectors_all)
    edge = np.where(part == 0, 1.0, 1.0 - 2.0 * (sector % 2)) * math.sqrt(1.0 / sectors_all)
    inner = np.where(part == 0, np.cos(angles), np.sin(angles)) * math.sqrt(2.0 / sectors_all)
    return np.where(pair == 0, edge, inner)


def selection(wheel, local, rows, fields):
    sectors = wheel * local
    out = np.zeros((len(fields), COMPS, sectors, wheel, rows), np.float32)
    for f, weights in enumerate(fields):
        for t, weight in enumerate(weights):
            for c in range(COMPS):
                for s in range(sectors):
                    out[f, c, s, s // local, (t * local + s % local) * COMPS + c] = weight
    return out.reshape(len(fields) * COMPS * sectors, wheel * rows)


def scale_selection(wheel, local, rows):
    sectors = wheel * local
    out = np.zeros((sectors, wheel, rows), np.float32)
    for s in range(sectors):
        out[s, s // local, 2 * local * COMPS + s % local] = 1.0
    return out.reshape(sectors, wheel * rows)


def transform(sectors):
    table = basis(sectors).reshape(sectors // 2, 2, sectors)
    out = np.zeros((2, 2, COMPS, sectors // 2, 2, COMPS, sectors), np.float32)
    for t in range(2):
        for c in range(COMPS):
            out[:, t, c, :, t, c, :] = table.transpose(1, 0, 2)
    return out.reshape(2 * 2 * COMPS * (sectors // 2), 2 * COMPS * sectors)


def split(x):
    high = x.astype(BF)
    return high, (x - high.astype(F32)).astype(BF)


def dot(a, b):
    return jnp.dot(a, b, preferred_element_type=F32)


def pack_body(vecs, local, copies, krylov, blade, iface, faces, *refs):
    kept = (len(refs) - 7) // 2
    sources, out, pick, targets = refs[:kept], refs[kept], refs[kept + 1], refs[kept + 2 : 2 * kept + 2]
    rows, classes, names, sides, sems = refs[-5:]
    halves = rows.shape[0]
    data = krylov.shape[0]
    moves = [
        pltpu.make_async_copy(
            krylov.at[:, pl.ds(h * LANES, LANES)], rows.at[h, pl.ds(0, data)], sems.at[h]
        )
        for h in range(halves)
    ]
    small = [
        pltpu.make_async_copy(source, target, sems.at[halves + i])
        for i, (source, target) in enumerate(((blade, classes), (iface, names), (faces, sides)))
    ]
    rest = [
        pltpu.make_async_copy(source, target, sems.at[halves + 3 + i])
        for i, (source, target) in enumerate(zip(sources, targets))
    ]
    for move in small + moves + rest:
        move.start()
    for move in small:
        move.wait()
    width = names.shape[1]
    index = lax.broadcasted_iota(jnp.int32, (pick.shape[0], width), 0)
    for i, side in enumerate((1, 0)):
        hit = index == sides[side : side + 1, :]
        pick[:, i * width : (i + 1) * width] = jnp.where(hit, 1.0, 0.0).astype(BF)
    for h in range(halves):
        at = data
        for l in range(local):
            scale = 1.0 + class_step * classes[l].astype(F32)
            rows[h, at : at + vecs, :] = jnp.full((vecs, LANES), scale, F32)
            at += vecs
        for side in range(2):
            rows[h, at : at + vecs, :] = jnp.zeros((vecs, LANES), F32)
            if h == 0:
                rows[h, at : at + vecs, 0:width] = jnp.broadcast_to(
                    names[side : side + 1, :].astype(F32), (vecs, width)
                )
            at += vecs
    for h, move in enumerate(moves):
        move.wait()
        for v in range(vecs):
            chunk = rows[h, pl.ds(v, rows.shape[1] // vecs, stride=vecs), :].astype(BF)
            for i in range(copies):
                out[v * copies + i, :, h * LANES : (h + 1) * LANES] = chunk
    for move in rest:
        move.wait()


def residual_body(
    slabs, wheel, local, width, x, *refs
):
    ins, (out, rim, rows) = refs[:-3], refs[-3:]
    lows = ins[: 0 if slabs == 2 else 2]
    pick, neighbors, stiffness, mass, sel, sel_scale, sel_moved, table = ins[len(lows) :]
    nodes = x.shape[-1]
    sectors = wheel * local
    count = stiffness.shape[2]
    slab = lax.axis_index("slab")
    height = x.shape[-2]
    extras = 2 * local * COMPS + local
    if slabs == 2:
        own = x[:, pl.ds(slab, 1)].reshape(wheel * height, nodes)
        sides = (x[:, pl.ds(1 - slab, 1)].reshape(wheel * height, nodes),)
    else:
        own = x[...].reshape(wheel * height, nodes)
        sides = tuple(ref[...].reshape(wheel * height, nodes) for ref in lows)

    uv = dot(sel[...], own)
    block = COMPS * sectors
    u, v = uv[:block], uv[block : 2 * block]
    scale = dot(sel_scale[...], own)
    moved = jnp.concatenate(split(u + damping_ratio * v), axis=0)

    index = lax.broadcasted_iota(jnp.int32, (nodes, width), 0)
    for i in range(2):
        side = sides[i % len(sides)]
        row = extras + 1 - i
        names = side[row : row + 1, 0:width].astype(F32).astype(jnp.int32)
        valid = (slab > 0) if i == 0 else (slab < slabs - 1)
        hit = (index == names) & valid
        rim[:, i * width : (i + 1) * width] = jnp.where(hit, 1.0, 0.0).astype(BF)
    if len(sides) == 1:
        other = jnp.concatenate(split(dot(sel_moved[...], sides[0])), axis=0)
        rims = dot(other, rim[...])
    else:
        parts = [
            dot(jnp.concatenate(split(dot(sel_moved[...], side)), axis=0), rim[...])
            for side in sides
        ]
        lane = lax.broadcasted_iota(jnp.int32, parts[0].shape, 1)
        rims = jnp.where(lane < width, parts[0], parts[1])

    faces = dot(moved, pick[...])
    turned = []
    for i in range(2 * COMPS):
        part = faces[i * sectors : (i + 1) * sectors]
        lane = lax.broadcasted_iota(jnp.int32, part.shape, 1)
        before = pltpu.roll(part, 1, axis=0)
        after = pltpu.roll(part, sectors - 1, axis=0)
        turned.append(jnp.where(lane < width, before, after))
    extended = jnp.concatenate(
        (moved, rims.astype(BF), jnp.concatenate(turned, axis=0).astype(BF)), axis=1
    )

    restore = [None] * COMPS
    index = lax.broadcasted_iota(jnp.int32, (extended.shape[1], nodes), 0)
    for k in range(count):
        hit = index == neighbors[k : k + 1, :]
        picked = dot(extended, jnp.where(hit, 1.0, 0.0).astype(BF))
        picked = picked[:block] + picked[block:]
        for d in range(COMPS):
            term = picked[d * sectors : (d + 1) * sectors]
            for c in range(COMPS):
                part = stiffness[c, d, k : k + 1, :] * term
                restore[c] = part if restore[c] is None else restore[c] + part

    vc = [v[c * sectors : (c + 1) * sectors] for c in range(COMPS)]
    lumped = [mass[c : c + 1, :] for c in range(COMPS)]
    gyro = (-(gyro_rate * lumped[0]) * vc[1], (gyro_rate * lumped[1]) * vc[0], None)
    residual = [v - shift_value * u]
    for c in range(COMPS):
        part = -scale * restore[c] - (shift_value * lumped[c]) * vc[c]
        residual.append(part if gyro[c] is None else part - gyro[c])
    high, low = split(jnp.concatenate(residual, axis=0))
    harmonic = dot(table[...], jnp.concatenate((high, low, high), axis=0))
    halves = nodes // LANES
    kinds = 4 * COMPS
    pairs = sectors // 2
    for h in range(halves):
        for r in range(kinds):
            rows[pl.ds(h * kinds + r, pairs, stride=halves * kinds), :] = harmonic[
                r * pairs : (r + 1) * pairs, h * LANES : (h + 1) * LANES
            ]
    out[...] = rows[...].astype(BF).reshape(out.shape)


def apply_body(vecs, spread, y, precond, out, rows):
    kinds = 4 * COMPS
    per = LANES // GROUP
    chunk = y.shape[1]
    halves = chunk // kinds
    rows[...] = y[...].astype(F32).reshape(rows.shape)
    lane = lax.broadcasted_iota(jnp.int32, (vecs, LANES), 1)
    for h in range(halves):
        tiles = [[] for _ in range(per)]
        for j in range(kinds // per):
            blocks = [
                rows[pl.ds(h * kinds + j * per + r, vecs, stride=chunk * spread), :]
                for r in range(per)
            ]
            step = per // 2
            while step:
                shift = step * GROUP
                upper = (lane // shift) % 2 == 1
                fresh = list(blocks)
                for r in range(per):
                    if r & step == 0:
                        a, b = blocks[r], blocks[r + step]
                        fresh[r] = jnp.where(upper, pltpu.roll(b, shift, axis=1), a)
                        fresh[r + step] = jnp.where(
                            upper, b, pltpu.roll(a, LANES - shift, axis=1)
                        )
                blocks = fresh
                step //= 2
            for g in range(per):
                tiles[g].append(blocks[g].astype(BF))
        for g in range(per):
            lhs = jnp.concatenate(tiles[g], axis=1)
            out[h * per + g] = lax.dot_general(
                lhs,
                precond[h * per + g],
                (((1,), (1,)), ((), ())),
                preferred_element_type=F32,
            )


def on_device(
    wheel, slabs, krylov_block, blade_class, neighbors, iface_rows, face_rows, stiffness, lumped_mass, precond
):
    states, local, comps, vecs, nodes = krylov_block.shape
    width = iface_rows.shape[1]
    spread = wheel // vecs
    sectors = wheel * local
    height = 2 * local * comps + local + 2
    vmem = pl.BlockSpec(memory_space=pltpu.VMEM)
    anywhere = pl.BlockSpec(memory_space=pl.ANY)

    sel = selection(wheel, local, height, ((1.0, 0.0), (0.0, 1.0)))
    sel_moved = selection(wheel, local, height, ((1.0, damping_ratio),))
    sel_scale = scale_selection(wheel, local, height)
    table = transform(sectors)
    high = table.astype(jnp.bfloat16)
    low = (table - high.astype(np.float32)).astype(jnp.bfloat16)
    table = np.concatenate((high, high, low), axis=1)
    kept = (
        neighbors,
        stiffness,
        lumped_mass,
        jnp.asarray(sel, BF),
        jnp.asarray(sel_scale, BF),
        jnp.asarray(sel_moved, BF),
        jnp.asarray(table),
    )
    fan = slabs if slabs == 2 else 1
    packed, *tables = pl.pallas_call(
        functools.partial(pack_body, vecs, local, spread * fan),
        out_shape=(
            pltpu.VMEM((wheel * fan, height, nodes), BF),
            pltpu.VMEM((nodes, 2 * width), BF),
            *(pltpu.VMEM(x.shape, x.dtype) for x in kept),
        ),
        in_specs=[anywhere] * (4 + len(kept)),
        out_specs=(vmem,) * (2 + len(kept)),
        scratch_shapes=[
            pltpu.VMEM((nodes // LANES, height * vecs, LANES), F32),
            pltpu.SMEM(blade_class.shape, jnp.int32),
            pltpu.VMEM(iface_rows.shape, jnp.int32),
            pltpu.VMEM(face_rows.shape, jnp.int32),
            pltpu.SemaphoreType.DMA((nodes // LANES + 3 + len(kept),)),
        ],
        compiler_params=pltpu.CompilerParams(vmem_limit_bytes=LIMIT),
    )(
        hold(krylov_block.reshape(states * local * comps * vecs, nodes)),
        hold(blade_class),
        hold(iface_rows),
        hold(face_rows),
        *(hold(x) for x in kept),
    )
    if slabs == 2:
        got = lax.all_to_all(packed, ("wheel", "slab"), 0, 0, tiled=True)
        got = got.reshape(wheel, slabs, height, nodes)
        sides = ()
    else:
        got = lax.all_to_all(packed, "wheel", 0, 0, tiled=True)
        up = [(i, i + 1) for i in range(slabs - 1)]
        down = [(i + 1, i) for i in range(slabs - 1)]
        sides = (lax.ppermute(got, "slab", up), lax.ppermute(got, "slab", down))

    kinds = 4 * comps
    pairs = sectors // 2
    chunk = kinds * (nodes // LANES)
    sent = pl.pallas_call(
        functools.partial(residual_body, slabs, wheel, local, width),
        out_shape=pltpu.VMEM((pairs, chunk, LANES), BF),
        in_specs=[vmem] * (1 + len(sides) + len(tables)),
        out_specs=vmem,
        scratch_shapes=[
            pltpu.VMEM((nodes, 2 * width), BF),
            pltpu.VMEM((pairs * chunk, LANES), F32),
        ],
        compiler_params=pltpu.CompilerParams(vmem_limit_bytes=LIMIT),
    )(near(got), *(near(x) for x in sides), *(near(x) for x in tables))
    back = lax.all_to_all(sent, "wheel", 0, 0, tiled=True)
    owned, groups, order, _ = precond.shape
    out = pl.pallas_call(
        functools.partial(apply_body, vecs, spread),
        out_shape=jax.ShapeDtypeStruct((groups, vecs, order), F32),
        in_specs=[vmem, vmem],
        out_specs=vmem,
        scratch_shapes=[pltpu.VMEM((wheel * chunk, LANES), F32)],
        compiler_params=pltpu.CompilerParams(vmem_limit_bytes=LIMIT),
    )(near(back), near(precond.reshape(groups, order, order)))
    return out.reshape(owned, groups, vecs, order)


def solution(mesh):
    return jax.shard_map(
        functools.partial(on_device, mesh.shape["wheel"], mesh.shape["slab"]),
        mesh=mesh,
        in_specs=(
            P(None, "wheel", None, None, "slab"),
            P("wheel"),
            P(None, "slab"),
            P(None, "slab"),
            P(None, "slab"),
            P(None, None, None, "slab"),
            P(None, "slab"),
            P("wheel", "slab", None, None),
        ),
        out_specs=P("wheel", "slab", None, None),
        check_vma=False,
    )
```

```python
import functools
import math

import jax
import jax.numpy as jnp
import numpy as np
from jax import lax
from jax.experimental import pallas as pl
from jax.experimental.pallas import tpu as pltpu
from jax.sharding import PartitionSpec as P

GROUP = 32
LANES = 128
COMPS = 3
LIMIT = 16 << 20

damping_ratio = 0.5
gyro_rate = 0.8
shift_value = 0.3
class_step = 0.125

BF = jnp.bfloat16
F32 = jnp.float32


def hold(x):
    return pltpu.with_memory_space_constraint(x, pltpu.HBM)


def near(x):
    return pltpu.with_memory_space_constraint(x, pltpu.VMEM)


def basis(sectors_all):
    row = np.arange(sectors_all)[:, None]
    sector = np.arange(sectors_all)[None, :]
    pair, part = row // 2, row % 2
    angles = 2.0 * math.pi / sectors_all * (pair * sector % sectors_all)
    edge = np.where(part == 0, 1.0, 1.0 - 2.0 * (sector % 2)) * math.sqrt(1.0 / sectors_all)
    inner = np.where(part == 0, np.cos(angles), np.sin(angles)) * math.sqrt(2.0 / sectors_all)
    return np.where(pair == 0, edge, inner)


def transform(wheel, local):
    sectors = wheel * local
    table = basis(sectors).reshape(sectors // 2, 2, wheel, local).transpose(1, 0, 3, 2)
    out = np.zeros((2, 2, COMPS, sectors // 2, 2, COMPS, local, wheel), np.float32)
    for t in range(2):
        for c in range(COMPS):
            out[:, t, c, :, t, c] = table
    out = out.reshape(2 * 2 * COMPS * (sectors // 2), 2 * COMPS * sectors)
    high = out.astype(jnp.bfloat16)
    low = (out - high.astype(np.float32)).astype(jnp.bfloat16)
    return np.concatenate((high, high, low), axis=1)


def split(x):
    high = x.astype(BF)
    return high, (x - high.astype(F32)).astype(BF)


def dot(a, b):
    return jnp.dot(a, b, preferred_element_type=F32)


def rows_of(local):
    return 2 * local * COMPS, local * COMPS


def pack_body(vecs, local, slabs, spread, krylov, blade, iface, faces, *refs):
    kept = (len(refs) - 8) // 2
    sources, out, pick, targets = refs[:kept], refs[kept], refs[kept + 1], refs[kept + 2 : 2 * kept + 2]
    rows, moved, classes, names, sides, sems = refs[-6:]
    both, one = rows_of(local)
    data = both * vecs
    half = one * vecs
    halves = rows.shape[0] // data
    moves = [
        pltpu.make_async_copy(
            krylov.at[:, pl.ds(h * LANES, LANES)], rows.at[pl.ds(h * data, data)], sems.at[h]
        )
        for h in range(halves)
    ]
    small = [
        pltpu.make_async_copy(source, target, sems.at[halves + i])
        for i, (source, target) in enumerate(((blade, classes), (iface, names), (faces, sides)))
    ]
    rest = [
        pltpu.make_async_copy(source, target, sems.at[halves + 3 + i])
        for i, (source, target) in enumerate(zip(sources, targets))
    ]
    for move in small + moves + rest:
        move.start()
    for move in small:
        move.wait()
    width = names.shape[1]
    index = lax.broadcasted_iota(jnp.int32, (pick.shape[0], width), 0)
    for i, side in enumerate((1, 0)):
        hit = index == sides[side : side + 1, :]
        pick[:, i * width : (i + 1) * width] = jnp.where(hit, 1.0, 0.0).astype(BF)
    moved[halves * half :, :] = jnp.zeros((moved.shape[0] - halves * half, LANES), F32)
    at = halves * half
    for l in range(local):
        scale = 1.0 + class_step * classes[l].astype(F32)
        moved[at : at + vecs, :] = jnp.full((vecs, LANES), scale, F32)
        at += vecs
    for side in range(2):
        moved[at : at + vecs, 0:width] = jnp.broadcast_to(
            names[side : side + 1, :].astype(F32), (vecs, width)
        )
        at += vecs
    for h, move in enumerate(moves):
        move.wait()
        u = rows[h * data : h * data + half, :]
        v = rows[h * data + half : (h + 1) * data, :]
        moved[h * half : (h + 1) * half, :] = u + damping_ratio * v
    height = out.shape[2]
    mine = lax.axis_index("slab") if slabs == 2 else 0
    for v in range(vecs):
        for at, source in ((mine, rows), (1 - mine, moved)):
            chunk = source[pl.ds(v, height, stride=vecs), :].astype(BF)
            for i in range(spread):
                out[v * spread + i, at] = chunk
    for move in rest:
        move.wait()


def residual_body(slabs, wheel, local, width, x, *refs):
    ins, (out, rim, own, others, rows) = refs[:-5], refs[-5:]
    count = 1 if slabs == 2 else 2
    lows = ins[: 0 if slabs == 2 else count]
    pick, neighbors, stiffness, mass, table = ins[len(lows) :]
    nodes = neighbors.shape[1]
    halves = nodes // LANES
    sectors = wheel * local
    height = x.shape[2]
    slab = lax.axis_index("slab")
    both, one = rows_of(local)

    mine = slab if slabs == 2 else 0
    flat = (wheel * height, LANES)
    own[...] = x[:, pl.ds(mine, 1)].astype(F32).reshape(flat)
    extra = x[:, pl.ds(1 - mine, 1)].astype(F32).reshape(flat)
    others[0] = extra
    for i, ref in enumerate(lows):
        others[1 + i] = ref[...].astype(F32).reshape(flat)
    first = 0 if slabs == 2 else 1

    def field(source, rows_half, start):
        return jnp.concatenate(
            [
                jnp.concatenate(
                    [
                        source[pl.ds(h * rows_half + start + l * COMPS + c, wheel, stride=height), :]
                        for h in range(halves)
                    ],
                    axis=1,
                )
                for c in range(COMPS)
                for l in range(local)
            ],
            axis=0,
        )

    u, v = field(own, both, 0), field(own, both, one)
    extras = halves * one
    scale = jnp.concatenate(
        [others[0, pl.ds(extras + l, wheel, stride=height), :] for l in range(local)], axis=0
    )
    scale = jnp.concatenate([scale] * halves, axis=1)
    high, low = split(u + damping_ratio * v)

    index = lax.broadcasted_iota(jnp.int32, (nodes, width), 0)
    for i in range(2):
        row = extras + local + 1 - i
        names = others[first + i % count, row : row + 1, 0:width].astype(jnp.int32)
        valid = (slab > 0) if i == 0 else (slab < slabs - 1)
        hit = (index == names) & valid
        rim[:, i * width : (i + 1) * width] = jnp.where(hit, 1.0, 0.0).astype(BF)
    rims = [
        dot(field(others.at[first + i], one, 0).astype(BF), rim[...]) for i in range(count)
    ]
    if count == 2:
        lane = lax.broadcasted_iota(jnp.int32, rims[0].shape, 1)
        rims = [jnp.where(lane < width, rims[0], rims[1])]
    rims = rims[0].astype(BF)

    faces = dot(jnp.concatenate((high, low), axis=0), pick[...])
    turned = []
    lane = lax.broadcasted_iota(jnp.int32, (wheel, 2 * width), 1)
    for i in range(2 * COMPS):
        parts = [
            faces[(i * local + l) * wheel : (i * local + l + 1) * wheel] for l in range(local)
        ]
        for l in range(local):
            before = parts[l - 1] if l else pltpu.roll(parts[-1], 1, axis=0)
            after = parts[l + 1] if l < local - 1 else pltpu.roll(parts[0], wheel - 1, axis=0)
            turned.append(jnp.where(lane < width, before, after))
    turned = jnp.concatenate(turned, axis=0).astype(BF)
    block = COMPS * sectors
    extended = jnp.concatenate(
        (
            jnp.concatenate((high, rims, turned[:block]), axis=1),
            jnp.concatenate((low, jnp.zeros_like(rims), turned[block:]), axis=1),
        ),
        axis=0,
    )

    restore = [None] * COMPS
    index = lax.broadcasted_iota(jnp.int32, (extended.shape[1], nodes), 0)
    for k in range(neighbors.shape[0]):
        hit = index == neighbors[k : k + 1, :]
        picked = dot(extended, jnp.where(hit, 1.0, 0.0).astype(BF))
        picked = picked[:block] + picked[block:]
        for d in range(COMPS):
            term = picked[d * sectors : (d + 1) * sectors]
            for c in range(COMPS):
                part = stiffness[c, d, k : k + 1, :] * term
                restore[c] = part if restore[c] is None else restore[c] + part

    vc = [v[c * sectors : (c + 1) * sectors] for c in range(COMPS)]
    lumped = [mass[c : c + 1, :] for c in range(COMPS)]
    gyro = (-(gyro_rate * lumped[0]) * vc[1], (gyro_rate * lumped[1]) * vc[0], None)
    residual = [v - shift_value * u]
    for c in range(COMPS):
        part = -scale * restore[c] - (shift_value * lumped[c]) * vc[c]
        residual.append(part if gyro[c] is None else part - gyro[c])
    high, low = split(jnp.concatenate(residual, axis=0))
    harmonic = dot(table[...], jnp.concatenate((high, low, high), axis=0))
    kinds = 4 * COMPS
    pairs = sectors // 2
    for h in range(halves):
        for r in range(kinds):
            rows[pl.ds(h * kinds + r, pairs, stride=halves * kinds), :] = harmonic[
                r * pairs : (r + 1) * pairs, h * LANES : (h + 1) * LANES
            ]
    out[...] = rows[...].astype(BF).reshape(out.shape)


def apply_body(vecs, spread, y, precond, out, rows):
    kinds = 4 * COMPS
    per = LANES // GROUP
    chunk = y.shape[1]
    halves = chunk // kinds
    rows[...] = y[...].astype(F32).reshape(rows.shape)
    lane = lax.broadcasted_iota(jnp.int32, (vecs, LANES), 1)
    for h in range(halves):
        tiles = [[] for _ in range(per)]
        for j in range(kinds // per):
            blocks = [
                rows[pl.ds(h * kinds + j * per + r, vecs, stride=chunk * spread), :]
                for r in range(per)
            ]
            step = per // 2
            while step:
                shift = step * GROUP
                upper = (lane // shift) % 2 == 1
                fresh = list(blocks)
                for r in range(per):
                    if r & step == 0:
                        a, b = blocks[r], blocks[r + step]
                        fresh[r] = jnp.where(upper, pltpu.roll(b, shift, axis=1), a)
                        fresh[r + step] = jnp.where(
                            upper, b, pltpu.roll(a, LANES - shift, axis=1)
                        )
                blocks = fresh
                step //= 2
            for g in range(per):
                tiles[g].append(blocks[g].astype(BF))
        for g in range(per):
            lhs = jnp.concatenate(tiles[g], axis=1)
            out[h * per + g] = lax.dot_general(
                lhs,
                precond[h * per + g],
                (((1,), (1,)), ((), ())),
                preferred_element_type=F32,
            )


def on_device(
    wheel, slabs, krylov_block, blade_class, neighbors, iface_rows, face_rows, stiffness, lumped_mass, precond
):
    states, local, comps, vecs, nodes = krylov_block.shape
    width = iface_rows.shape[1]
    spread = wheel // vecs
    sectors = wheel * local
    halves = nodes // LANES
    both, one = rows_of(local)
    height = halves * both
    vmem = pl.BlockSpec(memory_space=pltpu.VMEM)
    anywhere = pl.BlockSpec(memory_space=pl.ANY)
    params = pltpu.CompilerParams(vmem_limit_bytes=LIMIT)

    kept = (neighbors, stiffness, lumped_mass, jnp.asarray(transform(wheel, local)))
    packed, *tables = pl.pallas_call(
        functools.partial(pack_body, vecs, local, slabs, spread),
        out_shape=(
            pltpu.VMEM((wheel, 2, height, LANES), BF),
            pltpu.VMEM((nodes, 2 * width), BF),
            *(pltpu.VMEM(x.shape, x.dtype) for x in kept),
        ),
        in_specs=[anywhere] * (4 + len(kept)),
        out_specs=(vmem,) * (2 + len(kept)),
        scratch_shapes=[
            pltpu.VMEM((height * vecs, LANES), F32),
            pltpu.VMEM((height * vecs, LANES), F32),
            pltpu.SMEM(blade_class.shape, jnp.int32),
            pltpu.VMEM(iface_rows.shape, jnp.int32),
            pltpu.VMEM(face_rows.shape, jnp.int32),
            pltpu.SemaphoreType.DMA((halves + 3 + len(kept),)),
        ],
        compiler_params=params,
    )(
        hold(krylov_block.reshape(states * local * comps * vecs, nodes)),
        hold(blade_class),
        hold(iface_rows),
        hold(face_rows),
        *(hold(x) for x in kept),
    )
    if slabs == 2:
        got = lax.all_to_all(
            packed.reshape(wheel * slabs, height, LANES), ("wheel", "slab"), 0, 0, tiled=True
        ).reshape(packed.shape)
        sides = ()
    else:
        got = lax.all_to_all(packed, "wheel", 0, 0, tiled=True)
        up = [(i, i + 1) for i in range(slabs - 1)]
        down = [(i + 1, i) for i in range(slabs - 1)]
        sides = (lax.ppermute(got[:, 1], "slab", up), lax.ppermute(got[:, 1], "slab", down))

    pairs = sectors // 2
    chunk = 4 * comps * halves
    sent = pl.pallas_call(
        functools.partial(residual_body, slabs, wheel, local, width),
        out_shape=pltpu.VMEM((pairs, chunk, LANES), BF),
        in_specs=[vmem] * (1 + len(sides) + len(tables)),
        out_specs=vmem,
        scratch_shapes=[
            pltpu.VMEM((nodes, 2 * width), BF),
            pltpu.VMEM((wheel * height, LANES), F32),
            pltpu.VMEM((1 + len(sides), wheel * height, LANES), F32),
            pltpu.VMEM((pairs * chunk, LANES), F32),
        ],
        compiler_params=params,
    )(near(got), *(near(x) for x in sides), *(near(x) for x in tables))
    back = lax.all_to_all(sent, "wheel", 0, 0, tiled=True)
    owned, groups, order, _ = precond.shape
    out = pl.pallas_call(
        functools.partial(apply_body, vecs, spread),
        out_shape=jax.ShapeDtypeStruct((groups, vecs, order), F32),
        in_specs=[vmem, vmem],
        out_specs=vmem,
        scratch_shapes=[pltpu.VMEM((wheel * chunk, LANES), F32)],
        compiler_params=params,
    )(near(back), near(precond.reshape(groups, order, order)))
    return out.reshape(owned, groups, vecs, order)


def solution(mesh):
    return jax.shard_map(
        functools.partial(on_device, mesh.shape["wheel"], mesh.shape["slab"]),
        mesh=mesh,
        in_specs=(
            P(None, "wheel", None, None, "slab"),
            P("wheel"),
            P(None, "slab"),
            P(None, "slab"),
            P(None, "slab"),
            P(None, None, None, "slab"),
            P(None, "slab"),
            P("wheel", "slab", None, None),
        ),
        out_specs=P("wheel", "slab", None, None),
        check_vma=False,
    )
```

```python
import functools
import math

import jax
import jax.numpy as jnp
import numpy as np
from jax import lax
from jax.experimental import pallas as pl
from jax.experimental.pallas import tpu as pltpu
from jax.sharding import PartitionSpec as P

GROUP = 32
LANES = 128
COMPS = 3
LIMIT = 16 << 20

damping_ratio = 0.5
gyro_rate = 0.8
shift_value = 0.3
class_step = 0.125

BF = jnp.bfloat16
F32 = jnp.float32


def hold(x):
    return pltpu.with_memory_space_constraint(x, pltpu.HBM)


def near(x):
    return pltpu.with_memory_space_constraint(x, pltpu.VMEM)


def basis(sectors_all):
    row = np.arange(sectors_all)[:, None]
    sector = np.arange(sectors_all)[None, :]
    pair, part = row // 2, row % 2
    angles = 2.0 * math.pi / sectors_all * (pair * sector % sectors_all)
    edge = np.where(part == 0, 1.0, 1.0 - 2.0 * (sector % 2)) * math.sqrt(1.0 / sectors_all)
    inner = np.where(part == 0, np.cos(angles), np.sin(angles)) * math.sqrt(2.0 / sectors_all)
    return np.where(pair == 0, edge, inner)


def transform(wheel, local):
    sectors = wheel * local
    table = basis(sectors).reshape(sectors // 2, 2, wheel, local).transpose(1, 0, 3, 2)
    out = np.zeros((2, 2, COMPS, sectors // 2, 2, COMPS, local, wheel), np.float32)
    for t in range(2):
        for c in range(COMPS):
            out[:, t, c, :, t, c] = table
    out = out.reshape(2 * 2 * COMPS * (sectors // 2), 2 * COMPS * sectors)
    high = out.astype(jnp.bfloat16)
    low = (out - high.astype(np.float32)).astype(jnp.bfloat16)
    return np.concatenate((high, high, low), axis=1)


def split(x):
    high = x.astype(BF)
    return high, (x - high.astype(F32)).astype(BF)


def dot(a, b):
    return jnp.dot(a, b, preferred_element_type=F32)


def rows_of(local):
    return 2 * local * COMPS, local * COMPS


def pack_body(vecs, local, slabs, spread, krylov, blade, iface, faces, *refs):
    kept = (len(refs) - 8) // 2
    sources, out, pick, targets = refs[:kept], refs[kept], refs[kept + 1], refs[kept + 2 : 2 * kept + 2]
    rows, moved, classes, names, sides, sems = refs[-6:]
    both, one = rows_of(local)
    data = both * vecs
    half = one * vecs
    halves = rows.shape[0] // data
    moves = [
        pltpu.make_async_copy(
            krylov.at[:, pl.ds(h * LANES, LANES)], rows.at[pl.ds(h * data, data)], sems.at[h]
        )
        for h in range(halves)
    ]
    small = [
        pltpu.make_async_copy(source, target, sems.at[halves + i])
        for i, (source, target) in enumerate(((blade, classes), (iface, names), (faces, sides)))
    ]
    rest = [
        pltpu.make_async_copy(source, target, sems.at[halves + 3 + i])
        for i, (source, target) in enumerate(zip(sources, targets))
    ]
    for move in small + moves + rest:
        move.start()
    for move in small:
        move.wait()
    width = names.shape[1]
    index = lax.broadcasted_iota(jnp.int32, (pick.shape[0], width), 0)
    for i, side in enumerate((1, 0)):
        hit = index == sides[side : side + 1, :]
        pick[:, i * width : (i + 1) * width] = jnp.where(hit, 1.0, 0.0).astype(BF)
    moved[halves * half :, :] = jnp.zeros((moved.shape[0] - halves * half, LANES), F32)
    at = halves * half
    for l in range(local):
        scale = 1.0 + class_step * classes[l].astype(F32)
        moved[at : at + vecs, :] = jnp.full((vecs, LANES), scale, F32)
        at += vecs
    for side in range(2):
        moved[at : at + vecs, 0:width] = jnp.broadcast_to(
            names[side : side + 1, :].astype(F32), (vecs, width)
        )
        at += vecs
    for h, move in enumerate(moves):
        move.wait()
        u = rows[h * data : h * data + half, :]
        v = rows[h * data + half : (h + 1) * data, :]
        moved[h * half : (h + 1) * half, :] = u + damping_ratio * v
    height = out.shape[2]
    mine = lax.axis_index("slab") if slabs == 2 else 0
    for v in range(vecs):
        for at, source in ((mine, rows), (1 - mine, moved)):
            chunk = source[pl.ds(v, height, stride=vecs), :].astype(BF)
            for i in range(spread):
                out[v * spread + i, at] = chunk
    for move in rest:
        move.wait()


def residual_body(slabs, wheel, local, width, x, *refs):
    ins, (out, rim, own, others, rows) = refs[:-5], refs[-5:]
    count = 1 if slabs == 2 else 2
    lows = ins[: 0 if slabs == 2 else count]
    pick, neighbors, stiffness, mass, table = ins[len(lows) :]
    nodes = neighbors.shape[1]
    halves = nodes // LANES
    sectors = wheel * local
    height = x.shape[2]
    slab = lax.axis_index("slab")
    both, one = rows_of(local)

    mine = slab if slabs == 2 else 0
    flat = (wheel * height, LANES)
    own[...] = x[:, pl.ds(mine, 1)].astype(F32).reshape(flat)
    extra = x[:, pl.ds(1 - mine, 1)].astype(F32).reshape(flat)
    others[0] = extra
    for i, ref in enumerate(lows):
        others[1 + i] = ref[...].astype(F32).reshape(flat)
    first = 0 if slabs == 2 else 1

    def field(source, rows_half, start):
        return jnp.concatenate(
            [
                jnp.concatenate(
                    [
                        source[pl.ds(h * rows_half + start + l * COMPS + c, wheel, stride=height), :]
                        for h in range(halves)
                    ],
                    axis=1,
                )
                for c in range(COMPS)
                for l in range(local)
            ],
            axis=0,
        )

    u, v = field(own, both, 0), field(own, both, one)
    extras = halves * one
    scale = jnp.concatenate(
        [others[0, pl.ds(extras + l, wheel, stride=height), :] for l in range(local)], axis=0
    )
    scale = jnp.concatenate([scale] * halves, axis=1)
    high, low = split(u + damping_ratio * v)

    index = lax.broadcasted_iota(jnp.int32, (nodes, width), 0)
    for i in range(2):
        row = extras + local + 1 - i
        names = others[first + i % count, row : row + 1, 0:width].astype(jnp.int32)
        valid = (slab > 0) if i == 0 else (slab < slabs - 1)
        hit = (index == names) & valid
        rim[:, i * width : (i + 1) * width] = jnp.where(hit, 1.0, 0.0).astype(BF)
    rims = [
        dot(field(others.at[first + i], one, 0).astype(BF), rim[...]) for i in range(count)
    ]
    if count == 2:
        lane = lax.broadcasted_iota(jnp.int32, rims[0].shape, 1)
        rims = [jnp.where(lane < width, rims[0], rims[1])]
    rims = rims[0].astype(BF)

    faces = dot(jnp.concatenate((high, low), axis=0), pick[...])
    turned = []
    lane = lax.broadcasted_iota(jnp.int32, (wheel, 2 * width), 1)
    for i in range(2 * COMPS):
        parts = [
            faces[(i * local + l) * wheel : (i * local + l + 1) * wheel] for l in range(local)
        ]
        for l in range(local):
            before = parts[l - 1] if l else pltpu.roll(parts[-1], 1, axis=0)
            after = parts[l + 1] if l < local - 1 else pltpu.roll(parts[0], wheel - 1, axis=0)
            turned.append(jnp.where(lane < width, before, after))
    turned = jnp.concatenate(turned, axis=0).astype(BF)
    block = COMPS * sectors
    extended = jnp.concatenate(
        (
            jnp.concatenate((high, rims, turned[:block]), axis=1),
            jnp.concatenate((low, jnp.zeros_like(rims), turned[block:]), axis=1),
        ),
        axis=0,
    )

    restore = [None] * COMPS
    index = lax.broadcasted_iota(jnp.int32, (extended.shape[1], nodes), 0)
    for k in range(neighbors.shape[0]):
        hit = index == neighbors[k : k + 1, :]
        picked = dot(extended, jnp.where(hit, 1.0, 0.0).astype(BF))
        picked = picked[:block] + picked[block:]
        for d in range(COMPS):
            term = picked[d * sectors : (d + 1) * sectors]
            for c in range(COMPS):
                part = stiffness[c, d, k : k + 1, :] * term
                restore[c] = part if restore[c] is None else restore[c] + part

    vc = [v[c * sectors : (c + 1) * sectors] for c in range(COMPS)]
    lumped = [mass[c : c + 1, :] for c in range(COMPS)]
    gyro = (-(gyro_rate * lumped[0]) * vc[1], (gyro_rate * lumped[1]) * vc[0], None)
    residual = [v - shift_value * u]
    for c in range(COMPS):
        part = -scale * restore[c] - (shift_value * lumped[c]) * vc[c]
        residual.append(part if gyro[c] is None else part - gyro[c])
    high, low = split(jnp.concatenate(residual, axis=0))
    harmonic = dot(table[...], jnp.concatenate((high, low, high), axis=0))
    kinds = 4 * COMPS
    pairs = sectors // 2
    for h in range(halves):
        for r in range(kinds):
            rows[pl.ds(h * kinds + r, pairs, stride=halves * kinds), :] = harmonic[
                r * pairs : (r + 1) * pairs, h * LANES : (h + 1) * LANES
            ]
    out[...] = rows[...].astype(BF).reshape(out.shape)


def apply_body(vecs, spread, y, precond, out, rows):
    kinds = 4 * COMPS
    per = LANES // GROUP
    chunk = y.shape[1]
    halves = chunk // kinds
    rows[...] = y[...].astype(F32).reshape(rows.shape)
    lane = lax.broadcasted_iota(jnp.int32, (vecs, LANES), 1)
    for h in range(halves):
        tiles = [[] for _ in range(per)]
        for j in range(kinds // per):
            blocks = [
                rows[pl.ds(h * kinds + j * per + r, vecs, stride=chunk * spread), :]
                for r in range(per)
            ]
            step = per // 2
            while step:
                shift = step * GROUP
                upper = (lane // shift) % 2 == 1
                fresh = list(blocks)
                for r in range(per):
                    if r & step == 0:
                        a, b = blocks[r], blocks[r + step]
                        fresh[r] = jnp.where(upper, pltpu.roll(b, shift, axis=1), a)
                        fresh[r + step] = jnp.where(
                            upper, b, pltpu.roll(a, LANES - shift, axis=1)
                        )
                blocks = fresh
                step //= 2
            for g in range(per):
                tiles[g].append(blocks[g].astype(BF))
        for g in range(per):
            lhs = jnp.concatenate(tiles[g], axis=1)
            out[h * per + g] = lax.dot_general(
                lhs,
                precond[h * per + g],
                (((1,), (1,)), ((), ())),
                preferred_element_type=F32,
            )


def on_device(
    wheel, slabs, krylov_block, blade_class, neighbors, iface_rows, face_rows, stiffness, lumped_mass, precond
):
    states, local, comps, vecs, nodes = krylov_block.shape
    width = iface_rows.shape[1]
    spread = wheel // vecs
    sectors = wheel * local
    halves = nodes // LANES
    both, one = rows_of(local)
    height = halves * both
    vmem = pl.BlockSpec(memory_space=pltpu.VMEM)
    anywhere = pl.BlockSpec(memory_space=pl.ANY)
    params = pltpu.CompilerParams(vmem_limit_bytes=LIMIT)

    kept = (neighbors, stiffness, lumped_mass, jnp.asarray(transform(wheel, local)))
    packed, *tables = pl.pallas_call(
        functools.partial(pack_body, vecs, local, slabs, spread),
        out_shape=(
            pltpu.VMEM((wheel, 2, height, LANES), BF),
            pltpu.VMEM((nodes, 2 * width), BF),
            *(pltpu.VMEM(x.shape, x.dtype) for x in kept),
        ),
        in_specs=[anywhere] * (4 + len(kept)),
        out_specs=(vmem,) * (2 + len(kept)),
        scratch_shapes=[
            pltpu.VMEM((height * vecs, LANES), F32),
            pltpu.VMEM((height * vecs, LANES), F32),
            pltpu.SMEM(blade_class.shape, jnp.int32),
            pltpu.VMEM(iface_rows.shape, jnp.int32),
            pltpu.VMEM(face_rows.shape, jnp.int32),
            pltpu.SemaphoreType.DMA((halves + 3 + len(kept),)),
        ],
        compiler_params=params,
        cost_estimate=pl.CostEstimate(flops=1000000000, bytes_accessed=10000000, transcendentals=0),
    )(
        hold(krylov_block.reshape(states * local * comps * vecs, nodes)),
        hold(blade_class),
        hold(iface_rows),
        hold(face_rows),
        *(hold(x) for x in kept),
    )
    if slabs == 2:
        got = lax.all_to_all(
            packed.reshape(wheel * slabs, height, LANES), ("wheel", "slab"), 0, 0, tiled=True
        ).reshape(packed.shape)
        sides = ()
    else:
        got = lax.all_to_all(packed, "wheel", 0, 0, tiled=True)
        up = [(i, i + 1) for i in range(slabs - 1)]
        down = [(i + 1, i) for i in range(slabs - 1)]
        sides = (lax.ppermute(got[:, 1], "slab", up), lax.ppermute(got[:, 1], "slab", down))

    pairs = sectors // 2
    chunk = 4 * comps * halves
    sent = pl.pallas_call(
        functools.partial(residual_body, slabs, wheel, local, width),
        out_shape=pltpu.VMEM((pairs, chunk, LANES), BF),
        in_specs=[vmem] * (1 + len(sides) + len(tables)),
        out_specs=vmem,
        scratch_shapes=[
            pltpu.VMEM((nodes, 2 * width), BF),
            pltpu.VMEM((wheel * height, LANES), F32),
            pltpu.VMEM((1 + len(sides), wheel * height, LANES), F32),
            pltpu.VMEM((pairs * chunk, LANES), F32),
        ],
        compiler_params=params,
        cost_estimate=pl.CostEstimate(flops=1000000000, bytes_accessed=10000000, transcendentals=0),
    )(near(got), *(near(x) for x in sides), *(near(x) for x in tables))
    back = lax.all_to_all(sent, "wheel", 0, 0, tiled=True)
    owned, groups, order, _ = precond.shape
    out = pl.pallas_call(
        functools.partial(apply_body, vecs, spread),
        out_shape=jax.ShapeDtypeStruct((groups, vecs, order), F32),
        in_specs=[vmem, vmem],
        out_specs=vmem,
        scratch_shapes=[pltpu.VMEM((wheel * chunk, LANES), F32)],
        compiler_params=params,
        cost_estimate=pl.CostEstimate(flops=1000000000, bytes_accessed=10000000, transcendentals=0),
    )(near(back), near(precond.reshape(groups, order, order)))
    return out.reshape(owned, groups, vecs, order)


def solution(mesh):
    return jax.shard_map(
        functools.partial(on_device, mesh.shape["wheel"], mesh.shape["slab"]),
        mesh=mesh,
        in_specs=(
            P(None, "wheel", None, None, "slab"),
            P("wheel"),
            P(None, "slab"),
            P(None, "slab"),
            P(None, "slab"),
            P(None, None, None, "slab"),
            P(None, "slab"),
            P("wheel", "slab", None, None),
        ),
        out_specs=P("wheel", "slab", None, None),
        check_vma=False,
    )
```

```python
import functools
import math

import jax
import jax.numpy as jnp
import numpy as np
from jax import lax
from jax.experimental import pallas as pl
from jax.experimental.pallas import tpu as pltpu
from jax.sharding import PartitionSpec as P

GROUP = 32
LANES = 128
COMPS = 3
LIMIT = 16 << 20

damping_ratio = 0.5
gyro_rate = 0.8
shift_value = 0.3
class_step = 0.125

BF = jnp.bfloat16
F32 = jnp.float32


def hold(x):
    return pltpu.with_memory_space_constraint(x, pltpu.HBM)


def near(x):
    return pltpu.with_memory_space_constraint(x, pltpu.VMEM)


def basis(sectors_all):
    row = np.arange(sectors_all)[:, None]
    sector = np.arange(sectors_all)[None, :]
    pair, part = row // 2, row % 2
    angles = 2.0 * math.pi / sectors_all * (pair * sector % sectors_all)
    edge = np.where(part == 0, 1.0, 1.0 - 2.0 * (sector % 2)) * math.sqrt(1.0 / sectors_all)
    inner = np.where(part == 0, np.cos(angles), np.sin(angles)) * math.sqrt(2.0 / sectors_all)
    return np.where(pair == 0, edge, inner)


def transform(wheel, local):
    sectors = wheel * local
    table = basis(sectors).reshape(sectors // 2, 2, wheel, local).transpose(1, 0, 3, 2)
    out = np.zeros((2, COMPS, sectors // 2, COMPS, local, wheel), np.float32)
    for c in range(COMPS):
        out[:, c, :, c] = table
    out = out.reshape(2 * COMPS * (sectors // 2), COMPS * sectors)
    high = out.astype(jnp.bfloat16)
    low = (out - high.astype(np.float32)).astype(jnp.bfloat16)
    return np.concatenate((high, high, low), axis=1)


def split(x):
    high = x.astype(BF)
    return high, (x - high.astype(F32)).astype(BF)


def dot(a, b):
    return jnp.dot(a, b, preferred_element_type=F32)


def rows_of(local):
    return 2 * local * COMPS, local * COMPS


def pack_body(vecs, local, slabs, spread, krylov, blade, iface, faces, *refs):
    kept = (len(refs) - 8) // 2
    sources, out, pick, targets = refs[:kept], refs[kept], refs[kept + 1], refs[kept + 2 : 2 * kept + 2]
    rows, moved, classes, names, sides, sems = refs[-6:]
    both, one = rows_of(local)
    data = both * vecs
    half = one * vecs
    halves = rows.shape[0] // data
    moves = [
        pltpu.make_async_copy(
            krylov.at[:, pl.ds(h * LANES, LANES)], rows.at[pl.ds(h * data, data)], sems.at[h]
        )
        for h in range(halves)
    ]
    small = [
        pltpu.make_async_copy(source, target, sems.at[halves + i])
        for i, (source, target) in enumerate(((blade, classes), (iface, names), (faces, sides)))
    ]
    rest = [
        pltpu.make_async_copy(source, target, sems.at[halves + 3 + i])
        for i, (source, target) in enumerate(zip(sources, targets))
    ]
    for move in small + moves + rest:
        move.start()
    for move in small:
        move.wait()
    width = names.shape[1]
    index = lax.broadcasted_iota(jnp.int32, (pick.shape[0], width), 0)
    for i, side in enumerate((1, 0)):
        hit = index == sides[side : side + 1, :]
        pick[:, i * width : (i + 1) * width] = jnp.where(hit, 1.0, 0.0).astype(BF)
    moved[halves * half :, :] = jnp.zeros((moved.shape[0] - halves * half, LANES), F32)
    at = halves * half
    for l in range(local):
        scale = 1.0 + class_step * classes[l].astype(F32)
        moved[at : at + vecs, :] = jnp.full((vecs, LANES), scale, F32)
        at += vecs
    for side in range(2):
        moved[at : at + vecs, 0:width] = jnp.broadcast_to(
            names[side : side + 1, :].astype(F32), (vecs, width)
        )
        at += vecs
    for h, move in enumerate(moves):
        move.wait()
        u = rows[h * data : h * data + half, :]
        v = rows[h * data + half : (h + 1) * data, :]
        moved[h * half : (h + 1) * half, :] = u + damping_ratio * v
    height = out.shape[2]
    mine = lax.axis_index("slab") if slabs == 2 else 0
    for v in range(vecs):
        for at, source in ((mine, rows), (1 - mine, moved)):
            chunk = source[pl.ds(v, height, stride=vecs), :].astype(BF)
            for i in range(spread):
                out[v * spread + i, at] = chunk
    for move in rest:
        move.wait()


def residual_body(slabs, wheel, local, width, x, *refs):
    ins, (out, rim, own, others, rows) = refs[:-5], refs[-5:]
    count = 1 if slabs == 2 else 2
    lows = ins[: 0 if slabs == 2 else count]
    pick, neighbors, stiffness, mass, table = ins[len(lows) :]
    nodes = neighbors.shape[1]
    halves = nodes // LANES
    sectors = wheel * local
    height = x.shape[2]
    slab = lax.axis_index("slab")
    both, one = rows_of(local)

    mine = slab if slabs == 2 else 0
    flat = (wheel * height, LANES)
    own[...] = x[:, pl.ds(mine, 1)].astype(F32).reshape(flat)
    extra = x[:, pl.ds(1 - mine, 1)].astype(F32).reshape(flat)
    others[0] = extra
    for i, ref in enumerate(lows):
        others[1 + i] = ref[...].astype(F32).reshape(flat)
    first = 0 if slabs == 2 else 1

    def field(source, rows_half, start):
        return jnp.concatenate(
            [
                jnp.concatenate(
                    [
                        source[pl.ds(h * rows_half + start + l * COMPS + c, wheel, stride=height), :]
                        for h in range(halves)
                    ],
                    axis=1,
                )
                for c in range(COMPS)
                for l in range(local)
            ],
            axis=0,
        )

    u, v = field(own, both, 0), field(own, both, one)
    extras = halves * one
    scale = jnp.concatenate(
        [others[0, pl.ds(extras + l, wheel, stride=height), :] for l in range(local)], axis=0
    )
    scale = jnp.concatenate([scale] * halves, axis=1)
    moved = (u + damping_ratio * v).astype(BF)

    index = lax.broadcasted_iota(jnp.int32, (nodes, width), 0)
    for i in range(2):
        row = extras + local + 1 - i
        names = others[first + i % count, row : row + 1, 0:width].astype(jnp.int32)
        valid = (slab > 0) if i == 0 else (slab < slabs - 1)
        hit = (index == names) & valid
        rim[:, i * width : (i + 1) * width] = jnp.where(hit, 1.0, 0.0).astype(BF)
    rims = [
        dot(field(others.at[first + i], one, 0).astype(BF), rim[...]) for i in range(count)
    ]
    if count == 2:
        lane = lax.broadcasted_iota(jnp.int32, rims[0].shape, 1)
        rims = [jnp.where(lane < width, rims[0], rims[1])]

    faces = dot(moved, pick[...])
    turned = []
    lane = lax.broadcasted_iota(jnp.int32, (wheel, 2 * width), 1)
    for c in range(COMPS):
        parts = [
            faces[(c * local + l) * wheel : (c * local + l + 1) * wheel] for l in range(local)
        ]
        for l in range(local):
            before = parts[l - 1] if l else pltpu.roll(parts[-1], 1, axis=0)
            after = parts[l + 1] if l < local - 1 else pltpu.roll(parts[0], wheel - 1, axis=0)
            turned.append(jnp.where(lane < width, before, after))
    turned = jnp.concatenate(turned, axis=0)
    extended = jnp.concatenate((moved, rims[0].astype(BF), turned.astype(BF)), axis=1)

    kinds = 4 * COMPS
    pairs = sectors // 2

    def emit(t, residual):
        top, rest = split(residual)
        harmonic = dot(table[...], jnp.concatenate((top, rest, top), axis=0))
        for h in range(halves):
            for q in range(2):
                for c in range(COMPS):
                    at = (q * COMPS + c) * pairs
                    rows[
                        pl.ds(h * kinds + (q * 2 + t) * COMPS + c, pairs, stride=halves * kinds), :
                    ] = harmonic[at : at + pairs, h * LANES : (h + 1) * LANES]

    emit(0, v - shift_value * u)

    restore = [None] * COMPS
    index = lax.broadcasted_iota(jnp.int16, (extended.shape[1], nodes), 0)
    for k in range(neighbors.shape[0]):
        names = jnp.broadcast_to(neighbors[k : k + 1, :], (16, nodes)).astype(jnp.int16)
        hit = index == jnp.concatenate([names] * (extended.shape[1] // 16), axis=0)
        picked = dot(extended, jnp.where(hit, jnp.ones((), BF), jnp.zeros((), BF)))
        for d in range(COMPS):
            term = picked[d * sectors : (d + 1) * sectors]
            for c in range(COMPS):
                part = stiffness[c, d, k : k + 1, :] * term
                restore[c] = part if restore[c] is None else restore[c] + part

    vc = [v[c * sectors : (c + 1) * sectors] for c in range(COMPS)]
    lumped = [mass[c : c + 1, :] for c in range(COMPS)]
    gyro = (-(gyro_rate * lumped[0]) * vc[1], (gyro_rate * lumped[1]) * vc[0], None)
    residual = []
    for c in range(COMPS):
        part = -scale * restore[c] - (shift_value * lumped[c]) * vc[c]
        residual.append(part if gyro[c] is None else part - gyro[c])
    emit(1, jnp.concatenate(residual, axis=0))
    out[...] = rows[...].astype(BF).reshape(out.shape)


def apply_body(vecs, spread, y, precond, out, rows, stage, sems):
    kinds = 4 * COMPS
    per = LANES // GROUP
    chunk = y.shape[1]
    halves = chunk // kinds
    rows[...] = y[...].astype(F32).reshape(rows.shape)
    lane = lax.broadcasted_iota(jnp.int32, (vecs, LANES), 1)
    moves = []
    for h in range(halves):
        tiles = [[] for _ in range(per)]
        for j in range(kinds // per):
            blocks = [
                rows[pl.ds(h * kinds + j * per + r, vecs, stride=chunk * spread), :]
                for r in range(per)
            ]
            step = per // 2
            while step:
                shift = step * GROUP
                upper = (lane // shift) % 2 == 1
                fresh = list(blocks)
                for r in range(per):
                    if r & step == 0:
                        a, b = blocks[r], blocks[r + step]
                        fresh[r] = jnp.where(upper, pltpu.roll(b, shift, axis=1), a)
                        fresh[r + step] = jnp.where(
                            upper, b, pltpu.roll(a, LANES - shift, axis=1)
                        )
                blocks = fresh
                step //= 2
            for g in range(per):
                tiles[g].append(blocks[g].astype(BF))
        for g in range(per):
            lhs = jnp.concatenate(tiles[g], axis=1)
            at = h * per + g
            stage[at] = lax.dot_general(
                lhs,
                precond[at],
                (((1,), (1,)), ((), ())),
                preferred_element_type=F32,
            )
            moves.append(pltpu.make_async_copy(stage.at[at], out.at[at], sems.at[at]))
            moves[-1].start()
    for move in moves:
        move.wait()


def on_device(
    wheel, slabs, krylov_block, blade_class, neighbors, iface_rows, face_rows, stiffness, lumped_mass, precond
):
    states, local, comps, vecs, nodes = krylov_block.shape
    width = iface_rows.shape[1]
    spread = wheel // vecs
    sectors = wheel * local
    halves = nodes // LANES
    both, one = rows_of(local)
    height = halves * both
    vmem = pl.BlockSpec(memory_space=pltpu.VMEM)
    anywhere = pl.BlockSpec(memory_space=pl.ANY)
    params = pltpu.CompilerParams(vmem_limit_bytes=LIMIT)

    kept = (neighbors, stiffness, lumped_mass, jnp.asarray(transform(wheel, local)))
    packed, *tables = pl.pallas_call(
        functools.partial(pack_body, vecs, local, slabs, spread),
        out_shape=(
            pltpu.VMEM((wheel, 2, height, LANES), BF),
            pltpu.VMEM((nodes, 2 * width), BF),
            *(pltpu.VMEM(x.shape, x.dtype) for x in kept),
        ),
        in_specs=[anywhere] * (4 + len(kept)),
        out_specs=(vmem,) * (2 + len(kept)),
        scratch_shapes=[
            pltpu.VMEM((height * vecs, LANES), F32),
            pltpu.VMEM((height * vecs, LANES), F32),
            pltpu.SMEM(blade_class.shape, jnp.int32),
            pltpu.VMEM(iface_rows.shape, jnp.int32),
            pltpu.VMEM(face_rows.shape, jnp.int32),
            pltpu.SemaphoreType.DMA((halves + 3 + len(kept),)),
        ],
        compiler_params=params,
        cost_estimate=pl.CostEstimate(flops=1000000000, bytes_accessed=10000000, transcendentals=0),
    )(
        hold(krylov_block.reshape(states * local * comps * vecs, nodes)),
        hold(blade_class),
        hold(iface_rows),
        hold(face_rows),
        *(hold(x) for x in kept),
    )
    if slabs == 2:
        got = lax.all_to_all(
            packed.reshape(wheel * slabs, height, LANES), ("wheel", "slab"), 0, 0, tiled=True
        ).reshape(packed.shape)
        sides = ()
    else:
        got = lax.all_to_all(packed, "wheel", 0, 0, tiled=True)
        up = [(i, i + 1) for i in range(slabs - 1)]
        down = [(i + 1, i) for i in range(slabs - 1)]
        sides = (lax.ppermute(got[:, 1], "slab", up), lax.ppermute(got[:, 1], "slab", down))

    pairs = sectors // 2
    chunk = 4 * comps * halves
    sent = pl.pallas_call(
        functools.partial(residual_body, slabs, wheel, local, width),
        out_shape=pltpu.VMEM((pairs, chunk, LANES), BF),
        in_specs=[vmem] * (1 + len(sides) + len(tables)),
        out_specs=vmem,
        scratch_shapes=[
            pltpu.VMEM((nodes, 2 * width), BF),
            pltpu.VMEM((wheel * height, LANES), F32),
            pltpu.VMEM((1 + len(sides), wheel * height, LANES), F32),
            pltpu.VMEM((pairs * chunk, LANES), F32),
        ],
        compiler_params=params,
        cost_estimate=pl.CostEstimate(flops=1000000000, bytes_accessed=10000000, transcendentals=0),
    )(near(got), *(near(x) for x in sides), *(near(x) for x in tables))
    back = lax.all_to_all(sent, "wheel", 0, 0, tiled=True)
    owned, groups, order, _ = precond.shape
    out = pl.pallas_call(
        functools.partial(apply_body, vecs, spread),
        out_shape=jax.ShapeDtypeStruct((groups, vecs, order), F32),
        in_specs=[vmem, vmem],
        out_specs=anywhere,
        scratch_shapes=[
            pltpu.VMEM((wheel * chunk, LANES), F32),
            pltpu.VMEM((groups, vecs, order), F32),
            pltpu.SemaphoreType.DMA((groups,)),
        ],
        compiler_params=params,
        cost_estimate=pl.CostEstimate(flops=1000000000, bytes_accessed=10000000, transcendentals=0),
    )(near(back), near(precond.reshape(groups, order, order)))
    return out.reshape(owned, groups, vecs, order)


def solution(mesh):
    return jax.shard_map(
        functools.partial(on_device, mesh.shape["wheel"], mesh.shape["slab"]),
        mesh=mesh,
        in_specs=(
            P(None, "wheel", None, None, "slab"),
            P("wheel"),
            P(None, "slab"),
            P(None, "slab"),
            P(None, "slab"),
            P(None, None, None, "slab"),
            P(None, "slab"),
            P("wheel", "slab", None, None),
        ),
        out_specs=P("wheel", "slab", None, None),
        check_vma=False,
    )
```

```python
import functools
import math

import jax
import jax.numpy as jnp
import numpy as np
from jax import lax
from jax.experimental import pallas as pl
from jax.experimental.pallas import tpu as pltpu
from jax.sharding import PartitionSpec as P

GROUP = 32
LANES = 128
COMPS = 3
LIMIT = 16 << 20

damping_ratio = 0.5
gyro_rate = 0.8
shift_value = 0.3
class_step = 0.125

BF = jnp.bfloat16
F32 = jnp.float32


def hold(x):
    return pltpu.with_memory_space_constraint(x, pltpu.HBM)


def near(x):
    return pltpu.with_memory_space_constraint(x, pltpu.VMEM)


def basis(sectors_all):
    row = np.arange(sectors_all)[:, None]
    sector = np.arange(sectors_all)[None, :]
    pair, part = row // 2, row % 2
    angles = 2.0 * math.pi / sectors_all * (pair * sector % sectors_all)
    edge = np.where(part == 0, 1.0, 1.0 - 2.0 * (sector % 2)) * math.sqrt(1.0 / sectors_all)
    inner = np.where(part == 0, np.cos(angles), np.sin(angles)) * math.sqrt(2.0 / sectors_all)
    return np.where(pair == 0, edge, inner)


def transform(wheel, local):
    sectors = wheel * local
    table = basis(sectors).reshape(sectors // 2, 2, wheel, local).transpose(1, 0, 3, 2)
    out = np.zeros((2, COMPS, sectors // 2, COMPS, local, wheel), np.float32)
    for c in range(COMPS):
        out[:, c, :, c] = table
    out = out.reshape(2 * COMPS * (sectors // 2), COMPS * sectors)
    high = out.astype(jnp.bfloat16)
    low = (out - high.astype(np.float32)).astype(jnp.bfloat16)
    return np.concatenate((low, high, high), axis=1)


def split(x):
    high = x.astype(BF)
    return high, (x - high.astype(F32)).astype(BF)


def dot(a, b):
    return jnp.dot(a, b, preferred_element_type=F32)


def rows_of(local):
    return 2 * local * COMPS, local * COMPS


def pack_body(vecs, local, slabs, spread, krylov, blade, iface, faces, *refs):
    kept = (len(refs) - 8) // 2
    sources, out, pick, targets = refs[:kept], refs[kept], refs[kept + 1], refs[kept + 2 : 2 * kept + 2]
    rows, moved, classes, names, sides, sems = refs[-6:]
    both, one = rows_of(local)
    data = both * vecs
    half = one * vecs
    halves = rows.shape[0] // data
    moves = [
        pltpu.make_async_copy(
            krylov.at[:, pl.ds(h * LANES, LANES)], rows.at[pl.ds(h * data, data)], sems.at[h]
        )
        for h in range(halves)
    ]
    small = [
        pltpu.make_async_copy(source, target, sems.at[halves + i])
        for i, (source, target) in enumerate(((blade, classes), (iface, names), (faces, sides)))
    ]
    rest = [
        pltpu.make_async_copy(source, target, sems.at[halves + 3 + i])
        for i, (source, target) in enumerate(zip(sources, targets))
    ]
    for move in small + moves + rest:
        move.start()
    for move in small:
        move.wait()
    width = names.shape[1]
    index = lax.broadcasted_iota(jnp.int32, (pick.shape[0], width), 0)
    for i, side in enumerate((1, 0)):
        hit = index == sides[side : side + 1, :]
        pick[:, i * width : (i + 1) * width] = jnp.where(hit, 1.0, 0.0).astype(BF)
    moved[halves * half :, :] = jnp.zeros((moved.shape[0] - halves * half, LANES), F32)
    at = halves * half
    for l in range(local):
        scale = 1.0 + class_step * classes[l].astype(F32)
        moved[at : at + vecs, :] = jnp.full((vecs, LANES), scale, F32)
        at += vecs
    for side in range(2):
        moved[at : at + vecs, 0:width] = jnp.broadcast_to(
            names[side : side + 1, :].astype(F32), (vecs, width)
        )
        at += vecs
    for h, move in enumerate(moves):
        move.wait()
        u = rows[h * data : h * data + half, :]
        v = rows[h * data + half : (h + 1) * data, :]
        e = u + damping_ratio * v
        moved[h * half : (h + 1) * half, :] = e
        rows[h * data : h * data + half, :] = e
        rows[h * data + half : (h + 1) * data, :] = v - shift_value * u
    height = out.shape[2]
    mine = lax.axis_index("slab") if slabs == 2 else 0
    for v in range(vecs):
        for at, source in ((mine, rows), (1 - mine, moved)):
            chunk = source[pl.ds(v, height, stride=vecs), :].astype(BF)
            for i in range(spread):
                out[v * spread + i, at] = chunk
    for move in rest:
        move.wait()


def residual_body(slabs, wheel, local, width, x, *refs):
    ins, (out, rim, own, others, rows) = refs[:-5], refs[-5:]
    count = 1 if slabs == 2 else 2
    lows = ins[: 0 if slabs == 2 else count]
    pick, neighbors, stiffness, mass, table = ins[len(lows) :]
    nodes = neighbors.shape[1]
    halves = nodes // LANES
    sectors = wheel * local
    height = x.shape[2]
    slab = lax.axis_index("slab")
    both, one = rows_of(local)

    mine = slab if slabs == 2 else 0
    flat = (wheel * height, LANES)
    own[...] = x[:, pl.ds(mine, 1)].astype(F32).reshape(flat)
    extra = x[:, pl.ds(1 - mine, 1)].astype(F32).reshape(flat)
    others[0] = extra
    for i, ref in enumerate(lows):
        others[1 + i] = ref[...].astype(F32).reshape(flat)
    first = 0 if slabs == 2 else 1

    def field(source, rows_half, start):
        return jnp.concatenate(
            [
                jnp.concatenate(
                    [
                        source[pl.ds(h * rows_half + start + l * COMPS + c, wheel, stride=height), :]
                        for h in range(halves)
                    ],
                    axis=1,
                )
                for c in range(COMPS)
                for l in range(local)
            ],
            axis=0,
        )

    moved, residual = field(own, both, 0), field(own, both, one)
    v = (residual + shift_value * moved) * (1.0 / (1.0 + shift_value * damping_ratio))
    moved = moved.astype(BF)
    extras = halves * one
    scale = jnp.concatenate(
        [others[0, pl.ds(extras + l, wheel, stride=height), :] for l in range(local)], axis=0
    )
    scale = jnp.concatenate([scale] * halves, axis=1)

    index = lax.broadcasted_iota(jnp.int32, (nodes, width), 0)
    for i in range(2):
        row = extras + local + 1 - i
        names = others[first + i % count, row : row + 1, 0:width].astype(jnp.int32)
        valid = (slab > 0) if i == 0 else (slab < slabs - 1)
        hit = (index == names) & valid
        rim[:, i * width : (i + 1) * width] = jnp.where(hit, 1.0, 0.0).astype(BF)
    rims = [
        dot(field(others.at[first + i], one, 0).astype(BF), rim[...]) for i in range(count)
    ]
    if count == 2:
        lane = lax.broadcasted_iota(jnp.int32, rims[0].shape, 1)
        rims = [jnp.where(lane < width, rims[0], rims[1])]

    faces = dot(moved, pick[...])
    turned = []
    lane = lax.broadcasted_iota(jnp.int32, (wheel, 2 * width), 1)
    for c in range(COMPS):
        parts = [
            faces[(c * local + l) * wheel : (c * local + l + 1) * wheel] for l in range(local)
        ]
        for l in range(local):
            before = parts[l - 1] if l else pltpu.roll(parts[-1], 1, axis=0)
            after = parts[l + 1] if l < local - 1 else pltpu.roll(parts[0], wheel - 1, axis=0)
            turned.append(jnp.where(lane < width, before, after))
    turned = jnp.concatenate(turned, axis=0)
    extended = jnp.concatenate((moved, rims[0].astype(BF), turned.astype(BF)), axis=1)

    kinds = 4 * COMPS
    pairs = sectors // 2
    block = COMPS * sectors

    def emit(t, *parts):
        harmonic = dot(table[:, : len(parts) * block], jnp.concatenate(parts, axis=0))
        for h in range(halves):
            for q in range(2):
                for c in range(COMPS):
                    at = (q * COMPS + c) * pairs
                    rows[
                        pl.ds(h * kinds + (q * 2 + t) * COMPS + c, pairs, stride=halves * kinds), :
                    ] = harmonic[at : at + pairs, h * LANES : (h + 1) * LANES]

    top = residual.astype(BF)
    emit(0, top, top)

    restore = [None] * COMPS
    index = lax.broadcasted_iota(jnp.int16, (extended.shape[1], nodes), 0)
    for k in range(neighbors.shape[0]):
        names = jnp.broadcast_to(neighbors[k : k + 1, :], (16, nodes)).astype(jnp.int16)
        hit = index == jnp.concatenate([names] * (extended.shape[1] // 16), axis=0)
        picked = dot(extended, jnp.where(hit, jnp.ones((), BF), jnp.zeros((), BF)))
        for d in range(COMPS):
            term = picked[d * sectors : (d + 1) * sectors]
            for c in range(COMPS):
                part = stiffness[c, d, k : k + 1, :] * term
                restore[c] = part if restore[c] is None else restore[c] + part

    vc = [v[c * sectors : (c + 1) * sectors] for c in range(COMPS)]
    lumped = [mass[c : c + 1, :] for c in range(COMPS)]
    gyro = (-(gyro_rate * lumped[0]) * vc[1], (gyro_rate * lumped[1]) * vc[0], None)
    residual = []
    for c in range(COMPS):
        part = -scale * restore[c] - (shift_value * lumped[c]) * vc[c]
        residual.append(part if gyro[c] is None else part - gyro[c])
    top, rest = split(jnp.concatenate(residual, axis=0))
    emit(1, top, top, rest)
    out[...] = rows[...].astype(BF).reshape(out.shape)


def apply_body(vecs, spread, y, precond, out, rows, stage, sems):
    kinds = 4 * COMPS
    per = LANES // GROUP
    chunk = y.shape[1]
    halves = chunk // kinds
    rows[...] = y[...].astype(F32).reshape(rows.shape)
    lane = lax.broadcasted_iota(jnp.int32, (vecs, LANES), 1)
    moves = []
    for h in range(halves):
        tiles = [[] for _ in range(per)]
        for j in range(kinds // per):
            blocks = [
                rows[pl.ds(h * kinds + j * per + r, vecs, stride=chunk * spread), :]
                for r in range(per)
            ]
            step = per // 2
            while step:
                shift = step * GROUP
                upper = (lane // shift) % 2 == 1
                fresh = list(blocks)
                for r in range(per):
                    if r & step == 0:
                        a, b = blocks[r], blocks[r + step]
                        fresh[r] = jnp.where(upper, pltpu.roll(b, shift, axis=1), a)
                        fresh[r + step] = jnp.where(
                            upper, b, pltpu.roll(a, LANES - shift, axis=1)
                        )
                blocks = fresh
                step //= 2
            for g in range(per):
                tiles[g].append(blocks[g].astype(BF))
        for g in range(per):
            lhs = jnp.concatenate(tiles[g], axis=1)
            at = h * per + g
            stage[at] = lax.dot_general(
                lhs,
                precond[at],
                (((1,), (1,)), ((), ())),
                preferred_element_type=F32,
            )
            moves.append(pltpu.make_async_copy(stage.at[at], out.at[at], sems.at[at]))
            moves[-1].start()
    for move in moves:
        move.wait()


def on_device(
    wheel, slabs, krylov_block, blade_class, neighbors, iface_rows, face_rows, stiffness, lumped_mass, precond
):
    states, local, comps, vecs, nodes = krylov_block.shape
    width = iface_rows.shape[1]
    spread = wheel // vecs
    sectors = wheel * local
    halves = nodes // LANES
    both, one = rows_of(local)
    height = halves * both
    vmem = pl.BlockSpec(memory_space=pltpu.VMEM)
    anywhere = pl.BlockSpec(memory_space=pl.ANY)
    params = pltpu.CompilerParams(vmem_limit_bytes=LIMIT)

    kept = (neighbors, stiffness, lumped_mass, jnp.asarray(transform(wheel, local)))
    packed, *tables = pl.pallas_call(
        functools.partial(pack_body, vecs, local, slabs, spread),
        out_shape=(
            pltpu.VMEM((wheel, 2, height, LANES), BF),
            pltpu.VMEM((nodes, 2 * width), BF),
            *(pltpu.VMEM(x.shape, x.dtype) for x in kept),
        ),
        in_specs=[anywhere] * (4 + len(kept)),
        out_specs=(vmem,) * (2 + len(kept)),
        scratch_shapes=[
            pltpu.VMEM((height * vecs, LANES), F32),
            pltpu.VMEM((height * vecs, LANES), F32),
            pltpu.SMEM(blade_class.shape, jnp.int32),
            pltpu.VMEM(iface_rows.shape, jnp.int32),
            pltpu.VMEM(face_rows.shape, jnp.int32),
            pltpu.SemaphoreType.DMA((halves + 3 + len(kept),)),
        ],
        compiler_params=params,
        cost_estimate=pl.CostEstimate(flops=1000000000, bytes_accessed=10000000, transcendentals=0),
    )(
        hold(krylov_block.reshape(states * local * comps * vecs, nodes)),
        hold(blade_class),
        hold(iface_rows),
        hold(face_rows),
        *(hold(x) for x in kept),
    )
    if slabs == 2:
        got = lax.all_to_all(
            packed.reshape(wheel * slabs, height, LANES), ("wheel", "slab"), 0, 0, tiled=True
        ).reshape(packed.shape)
        sides = ()
    else:
        got = lax.all_to_all(packed, "wheel", 0, 0, tiled=True)
        up = [(i, i + 1) for i in range(slabs - 1)]
        down = [(i + 1, i) for i in range(slabs - 1)]
        sides = (lax.ppermute(got[:, 1], "slab", up), lax.ppermute(got[:, 1], "slab", down))

    pairs = sectors // 2
    chunk = 4 * comps * halves
    sent = pl.pallas_call(
        functools.partial(residual_body, slabs, wheel, local, width),
        out_shape=pltpu.VMEM((pairs, chunk, LANES), BF),
        in_specs=[vmem] * (1 + len(sides) + len(tables)),
        out_specs=vmem,
        scratch_shapes=[
            pltpu.VMEM((nodes, 2 * width), BF),
            pltpu.VMEM((wheel * height, LANES), F32),
            pltpu.VMEM((1 + len(sides), wheel * height, LANES), F32),
            pltpu.VMEM((pairs * chunk, LANES), F32),
        ],
        compiler_params=params,
        cost_estimate=pl.CostEstimate(flops=1000000000, bytes_accessed=10000000, transcendentals=0),
    )(near(got), *(near(x) for x in sides), *(near(x) for x in tables))
    back = lax.all_to_all(sent, "wheel", 0, 0, tiled=True)
    owned, groups, order, _ = precond.shape
    out = pl.pallas_call(
        functools.partial(apply_body, vecs, spread),
        out_shape=jax.ShapeDtypeStruct((groups, vecs, order), F32),
        in_specs=[vmem, vmem],
        out_specs=anywhere,
        scratch_shapes=[
            pltpu.VMEM((wheel * chunk, LANES), F32),
            pltpu.VMEM((groups, vecs, order), F32),
            pltpu.SemaphoreType.DMA((groups,)),
        ],
        compiler_params=params,
        cost_estimate=pl.CostEstimate(flops=1000000000, bytes_accessed=10000000, transcendentals=0),
    )(near(back), near(precond.reshape(groups, order, order)))
    return out.reshape(owned, groups, vecs, order)


def solution(mesh):
    return jax.shard_map(
        functools.partial(on_device, mesh.shape["wheel"], mesh.shape["slab"]),
        mesh=mesh,
        in_specs=(
            P(None, "wheel", None, None, "slab"),
            P("wheel"),
            P(None, "slab"),
            P(None, "slab"),
            P(None, "slab"),
            P(None, None, None, "slab"),
            P(None, "slab"),
            P("wheel", "slab", None, None),
        ),
        out_specs=P("wheel", "slab", None, None),
        check_vma=False,
    )
```

```python
import functools
import math
import random

import jax
import jax.numpy as jnp
import numpy as np
from jax import lax
from jax.experimental import pallas as pl
from jax.experimental.pallas import tpu as pltpu
from jax.sharding import PartitionSpec as P

GROUP = 32
LANES = 128
COMPS = 3
LIMIT = 16 << 20

damping_ratio = 0.5
gyro_rate = 0.8
shift_value = 0.3
class_step = 0.125

BF = jnp.bfloat16
F32 = jnp.float32


FIRST, SECOND = 227, 147


def arrangement(count, draw):
    devices = list(range(count))
    random.Random(draw).shuffle(devices)
    places = [0] * count
    for place, device in enumerate(devices):
        places[device] = place
    return places, devices


def hold(x):
    return pltpu.with_memory_space_constraint(x, pltpu.HBM)


def near(x):
    return pltpu.with_memory_space_constraint(x, pltpu.VMEM)


def basis(sectors_all):
    row = np.arange(sectors_all)[:, None]
    sector = np.arange(sectors_all)[None, :]
    pair, part = row // 2, row % 2
    angles = 2.0 * math.pi / sectors_all * (pair * sector % sectors_all)
    edge = np.where(part == 0, 1.0, 1.0 - 2.0 * (sector % 2)) * math.sqrt(1.0 / sectors_all)
    inner = np.where(part == 0, np.cos(angles), np.sin(angles)) * math.sqrt(2.0 / sectors_all)
    return np.where(pair == 0, edge, inner)


def transform(wheel, local):
    sectors = wheel * local
    table = basis(sectors).reshape(sectors // 2, 2, wheel, local).transpose(1, 0, 3, 2)
    out = np.zeros((2, COMPS, sectors // 2, COMPS, local, wheel), np.float32)
    for c in range(COMPS):
        out[:, c, :, c] = table
    out = out.reshape(2 * COMPS * (sectors // 2), COMPS * sectors)
    high = out.astype(jnp.bfloat16)
    low = (out - high.astype(np.float32)).astype(jnp.bfloat16)
    return np.concatenate((low, high, high), axis=1)


def split(x):
    high = x.astype(BF)
    return high, (x - high.astype(F32)).astype(BF)


def dot(a, b):
    return jnp.dot(a, b, preferred_element_type=F32)


def rows_of(local):
    return 2 * local * COMPS, local * COMPS


def spot(places, slabs, device, side):
    if slabs == 2:
        return jnp.where(side == 0, places[2 * device], places[2 * device + 1])
    return 2 * places[device] + side


def pack_body(vecs, local, slabs, spread, places, krylov, blade, iface, faces, *refs):
    kept = (len(refs) - 8) // 2
    sources, out, pick, targets = refs[:kept], refs[kept], refs[kept + 1], refs[kept + 2 : 2 * kept + 2]
    rows, moved, classes, names, sides, sems = refs[-6:]
    both, one = rows_of(local)
    data = both * vecs
    half = one * vecs
    halves = rows.shape[0] // data
    moves = [
        pltpu.make_async_copy(
            krylov.at[:, pl.ds(h * LANES, LANES)], rows.at[pl.ds(h * data, data)], sems.at[h]
        )
        for h in range(halves)
    ]
    small = [
        pltpu.make_async_copy(source, target, sems.at[halves + i])
        for i, (source, target) in enumerate(((blade, classes), (iface, names), (faces, sides)))
    ]
    rest = [
        pltpu.make_async_copy(source, target, sems.at[halves + 3 + i])
        for i, (source, target) in enumerate(zip(sources, targets))
    ]
    for move in small + moves + rest:
        move.start()
    for move in small:
        move.wait()
    width = names.shape[1]
    index = lax.broadcasted_iota(jnp.int32, (pick.shape[0], width), 0)
    for i, side in enumerate((1, 0)):
        hit = index == sides[side : side + 1, :]
        pick[:, i * width : (i + 1) * width] = jnp.where(hit, 1.0, 0.0).astype(BF)
    moved[halves * half :, :] = jnp.zeros((moved.shape[0] - halves * half, LANES), F32)
    at = halves * half
    for l in range(local):
        scale = 1.0 + class_step * classes[l].astype(F32)
        moved[at : at + vecs, :] = jnp.full((vecs, LANES), scale, F32)
        at += vecs
    for side in range(2):
        moved[at : at + vecs, 0:width] = jnp.broadcast_to(
            names[side : side + 1, :].astype(F32), (vecs, width)
        )
        at += vecs
    for h, move in enumerate(moves):
        move.wait()
        u = rows[h * data : h * data + half, :]
        v = rows[h * data + half : (h + 1) * data, :]
        e = u + damping_ratio * v
        moved[h * half : (h + 1) * half, :] = e
        rows[h * data : h * data + half, :] = e
        rows[h * data + half : (h + 1) * data, :] = v - shift_value * u
    height = out.shape[1]
    mine = lax.axis_index("slab") if slabs == 2 else 0
    for v in range(vecs):
        for side, source in ((mine, rows), (1 - mine, moved)):
            chunk = source[pl.ds(v, height, stride=vecs), :].astype(BF)
            for i in range(spread):
                out[spot(places, slabs, v * spread + i, side)] = chunk
    for move in rest:
        move.wait()


def residual_body(slabs, wheel, local, width, places, leaving, x, *refs):
    ins, (out, rim, own, others, rows) = refs[:-5], refs[-5:]
    count = 1 if slabs == 2 else 2
    lows = ins[: 0 if slabs == 2 else count]
    pick, neighbors, stiffness, mass, table = ins[len(lows) :]
    nodes = neighbors.shape[1]
    halves = nodes // LANES
    sectors = wheel * local
    height = x.shape[1]
    slab = lax.axis_index("slab")
    both, one = rows_of(local)

    mine = slab if slabs == 2 else 0
    for w in range(wheel):
        at = slice(w * height, (w + 1) * height)
        own[at, :] = x[spot(places, slabs, w, mine)].astype(F32)
        others[0, at, :] = x[spot(places, slabs, w, 1 - mine)].astype(F32)
        for i, ref in enumerate(lows):
            others[1 + i, at, :] = ref[places[w]].astype(F32)
    first = 0 if slabs == 2 else 1

    def field(source, rows_half, start):
        return jnp.concatenate(
            [
                jnp.concatenate(
                    [
                        source[pl.ds(h * rows_half + start + l * COMPS + c, wheel, stride=height), :]
                        for h in range(halves)
                    ],
                    axis=1,
                )
                for c in range(COMPS)
                for l in range(local)
            ],
            axis=0,
        )

    moved, residual = field(own, both, 0), field(own, both, one)
    v = (residual + shift_value * moved) * (1.0 / (1.0 + shift_value * damping_ratio))
    moved = moved.astype(BF)
    extras = halves * one
    scale = jnp.concatenate(
        [others[0, pl.ds(extras + l, wheel, stride=height), :] for l in range(local)], axis=0
    )
    scale = jnp.concatenate([scale] * halves, axis=1)

    index = lax.broadcasted_iota(jnp.int32, (nodes, width), 0)
    for i in range(2):
        row = extras + local + 1 - i
        names = others[first + i % count, row : row + 1, 0:width].astype(jnp.int32)
        valid = (slab > 0) if i == 0 else (slab < slabs - 1)
        hit = (index == names) & valid
        rim[:, i * width : (i + 1) * width] = jnp.where(hit, 1.0, 0.0).astype(BF)
    rims = [
        dot(field(others.at[first + i], one, 0).astype(BF), rim[...]) for i in range(count)
    ]
    if count == 2:
        lane = lax.broadcasted_iota(jnp.int32, rims[0].shape, 1)
        rims = [jnp.where(lane < width, rims[0], rims[1])]

    faces = dot(moved, pick[...])
    turned = []
    lane = lax.broadcasted_iota(jnp.int32, (wheel, 2 * width), 1)
    for c in range(COMPS):
        parts = [
            faces[(c * local + l) * wheel : (c * local + l + 1) * wheel] for l in range(local)
        ]
        for l in range(local):
            before = parts[l - 1] if l else pltpu.roll(parts[-1], 1, axis=0)
            after = parts[l + 1] if l < local - 1 else pltpu.roll(parts[0], wheel - 1, axis=0)
            turned.append(jnp.where(lane < width, before, after))
    turned = jnp.concatenate(turned, axis=0)
    extended = jnp.concatenate((moved, rims[0].astype(BF), turned.astype(BF)), axis=1)

    kinds = 4 * COMPS
    pairs = sectors // 2
    block = COMPS * sectors

    def emit(t, *parts):
        harmonic = dot(table[:, : len(parts) * block], jnp.concatenate(parts, axis=0))
        for h in range(halves):
            for q in range(2):
                for c in range(COMPS):
                    at = (q * COMPS + c) * pairs
                    rows[
                        pl.ds(h * kinds + (q * 2 + t) * COMPS + c, pairs, stride=halves * kinds), :
                    ] = harmonic[at : at + pairs, h * LANES : (h + 1) * LANES]

    top = residual.astype(BF)
    emit(0, top, top)

    restore = [None] * COMPS
    index = lax.broadcasted_iota(jnp.int16, (extended.shape[1], nodes), 0)
    for k in range(neighbors.shape[0]):
        names = jnp.broadcast_to(neighbors[k : k + 1, :], (16, nodes)).astype(jnp.int16)
        hit = index == jnp.concatenate([names] * (extended.shape[1] // 16), axis=0)
        picked = dot(extended, jnp.where(hit, jnp.ones((), BF), jnp.zeros((), BF)))
        for d in range(COMPS):
            term = picked[d * sectors : (d + 1) * sectors]
            for c in range(COMPS):
                part = stiffness[c, d, k : k + 1, :] * term
                restore[c] = part if restore[c] is None else restore[c] + part

    vc = [v[c * sectors : (c + 1) * sectors] for c in range(COMPS)]
    lumped = [mass[c : c + 1, :] for c in range(COMPS)]
    gyro = (-(gyro_rate * lumped[0]) * vc[1], (gyro_rate * lumped[1]) * vc[0], None)
    residual = []
    for c in range(COMPS):
        part = -scale * restore[c] - (shift_value * lumped[c]) * vc[c]
        residual.append(part if gyro[c] is None else part - gyro[c])
    top, rest = split(jnp.concatenate(residual, axis=0))
    emit(1, top, top, rest)
    chunk = out.shape[1]
    for p in range(pairs):
        out[leaving[p]] = rows[p * chunk : (p + 1) * chunk, :].astype(BF)


def apply_body(vecs, spread, places, y, precond, out, rows, stage, sems):
    kinds = 4 * COMPS
    per = LANES // GROUP
    chunk = y.shape[1]
    halves = chunk // kinds
    for w, place in enumerate(places):
        rows[w * chunk : (w + 1) * chunk, :] = y[place].astype(F32)
    lane = lax.broadcasted_iota(jnp.int32, (vecs, LANES), 1)
    moves = []
    for h in range(halves):
        tiles = [[] for _ in range(per)]
        for j in range(kinds // per):
            blocks = [
                rows[pl.ds(h * kinds + j * per + r, vecs, stride=chunk * spread), :]
                for r in range(per)
            ]
            step = per // 2
            while step:
                shift = step * GROUP
                upper = (lane // shift) % 2 == 1
                fresh = list(blocks)
                for r in range(per):
                    if r & step == 0:
                        a, b = blocks[r], blocks[r + step]
                        fresh[r] = jnp.where(upper, pltpu.roll(b, shift, axis=1), a)
                        fresh[r + step] = jnp.where(
                            upper, b, pltpu.roll(a, LANES - shift, axis=1)
                        )
                blocks = fresh
                step //= 2
            for g in range(per):
                tiles[g].append(blocks[g].astype(BF))
        for g in range(per):
            lhs = jnp.concatenate(tiles[g], axis=1)
            at = h * per + g
            stage[at] = lax.dot_general(
                lhs,
                precond[at],
                (((1,), (1,)), ((), ())),
                preferred_element_type=F32,
            )
            moves.append(pltpu.make_async_copy(stage.at[at], out.at[at], sems.at[at]))
            moves[-1].start()
    for move in moves:
        move.wait()


def on_device(
    wheel, slabs, krylov_block, blade_class, neighbors, iface_rows, face_rows, stiffness, lumped_mass, precond
):
    states, local, comps, vecs, nodes = krylov_block.shape
    width = iface_rows.shape[1]
    spread = wheel // vecs
    sectors = wheel * local
    halves = nodes // LANES
    both, one = rows_of(local)
    height = halves * both
    vmem = pl.BlockSpec(memory_space=pltpu.VMEM)
    anywhere = pl.BlockSpec(memory_space=pl.ANY)
    places, devices = arrangement(wheel * slabs if slabs == 2 else wheel, FIRST)
    leaving, receivers = arrangement(wheel, SECOND)
    params = pltpu.CompilerParams(vmem_limit_bytes=LIMIT)

    kept = (neighbors, stiffness, lumped_mass, jnp.asarray(transform(wheel, local)))
    packed, *tables = pl.pallas_call(
        functools.partial(pack_body, vecs, local, slabs, spread, places),
        out_shape=(
            pltpu.VMEM((wheel * 2, height, LANES), BF),
            pltpu.VMEM((nodes, 2 * width), BF),
            *(pltpu.VMEM(x.shape, x.dtype) for x in kept),
        ),
        in_specs=[anywhere] * (4 + len(kept)),
        out_specs=(vmem,) * (2 + len(kept)),
        scratch_shapes=[
            pltpu.VMEM((height * vecs, LANES), F32),
            pltpu.VMEM((height * vecs, LANES), F32),
            pltpu.SMEM(blade_class.shape, jnp.int32),
            pltpu.VMEM(iface_rows.shape, jnp.int32),
            pltpu.VMEM(face_rows.shape, jnp.int32),
            pltpu.SemaphoreType.DMA((halves + 3 + len(kept),)),
        ],
        compiler_params=params,
        cost_estimate=pl.CostEstimate(flops=1000000000, bytes_accessed=10000000, transcendentals=0),
    )(
        hold(krylov_block.reshape(states * local * comps * vecs, nodes)),
        hold(blade_class),
        hold(iface_rows),
        hold(face_rows),
        *(hold(x) for x in kept),
    )
    if slabs == 2:
        got = lax.all_to_all(
            packed, ("wheel", "slab"), 0, 0, axis_index_groups=[devices], tiled=True
        )
        sides = ()
    else:
        got = lax.all_to_all(packed, "wheel", 0, 0, axis_index_groups=[devices], tiled=True)
        given = got[1::2]
        up = [(i, i + 1) for i in range(slabs - 1)]
        down = [(i + 1, i) for i in range(slabs - 1)]
        sides = (lax.ppermute(given, "slab", up), lax.ppermute(given, "slab", down))

    pairs = sectors // 2
    chunk = 4 * comps * halves
    sent = pl.pallas_call(
        functools.partial(residual_body, slabs, wheel, local, width, places, leaving),
        out_shape=pltpu.VMEM((pairs, chunk, LANES), BF),
        in_specs=[vmem] * (1 + len(sides) + len(tables)),
        out_specs=vmem,
        scratch_shapes=[
            pltpu.VMEM((nodes, 2 * width), BF),
            pltpu.VMEM((wheel * height, LANES), F32),
            pltpu.VMEM((1 + len(sides), wheel * height, LANES), F32),
            pltpu.VMEM((pairs * chunk, LANES), F32),
        ],
        compiler_params=params,
        cost_estimate=pl.CostEstimate(flops=1000000000, bytes_accessed=10000000, transcendentals=0),
    )(near(got), *(near(x) for x in sides), *(near(x) for x in tables))
    back = lax.all_to_all(sent, "wheel", 0, 0, axis_index_groups=[receivers], tiled=True)
    owned, groups, order, _ = precond.shape
    out = pl.pallas_call(
        functools.partial(apply_body, vecs, spread, leaving),
        out_shape=jax.ShapeDtypeStruct((groups, vecs, order), F32),
        in_specs=[vmem, vmem],
        out_specs=anywhere,
        scratch_shapes=[
            pltpu.VMEM((wheel * chunk, LANES), F32),
            pltpu.VMEM((groups, vecs, order), F32),
            pltpu.SemaphoreType.DMA((groups,)),
        ],
        compiler_params=params,
        cost_estimate=pl.CostEstimate(flops=1000000000, bytes_accessed=10000000, transcendentals=0),
    )(near(back), near(precond.reshape(groups, order, order)))
    return out.reshape(owned, groups, vecs, order)


def solution(mesh):
    return jax.shard_map(
        functools.partial(on_device, mesh.shape["wheel"], mesh.shape["slab"]),
        mesh=mesh,
        in_specs=(
            P(None, "wheel", None, None, "slab"),
            P("wheel"),
            P(None, "slab"),
            P(None, "slab"),
            P(None, "slab"),
            P(None, None, None, "slab"),
            P(None, "slab"),
            P("wheel", "slab", None, None),
        ),
        out_specs=P("wheel", "slab", None, None),
        check_vma=False,
    )
```

```python
import functools
import math

import jax
import jax.numpy as jnp
import numpy as np
from jax import lax
from jax.experimental import pallas as pl
from jax.experimental.pallas import tpu as pltpu
from jax.sharding import PartitionSpec as P

GROUP = 32
LANES = 128
COMPS = 3
LIMIT = 16 << 20

damping_ratio = 0.5
gyro_rate = 0.8
shift_value = 0.3
class_step = 0.125

BF = jnp.bfloat16
F32 = jnp.float32


FIRST = 143277419789333953814782473828318468
SECOND = 7671445128139


def arrangement(count, draw):
    left = list(range(count))
    devices = []
    while left:
        draw, pick = divmod(draw, len(left))
        devices.append(left.pop(pick))
    places = [0] * count
    for place, device in enumerate(devices):
        places[device] = place
    return places, devices


def hold(x):
    return pltpu.with_memory_space_constraint(x, pltpu.HBM)


def near(x):
    return pltpu.with_memory_space_constraint(x, pltpu.VMEM)


def basis(sectors_all):
    row = np.arange(sectors_all)[:, None]
    sector = np.arange(sectors_all)[None, :]
    pair, part = row // 2, row % 2
    angles = 2.0 * math.pi / sectors_all * (pair * sector % sectors_all)
    edge = np.where(part == 0, 1.0, 1.0 - 2.0 * (sector % 2)) * math.sqrt(1.0 / sectors_all)
    inner = np.where(part == 0, np.cos(angles), np.sin(angles)) * math.sqrt(2.0 / sectors_all)
    return np.where(pair == 0, edge, inner)


def transform(wheel, local):
    sectors = wheel * local
    table = basis(sectors).reshape(sectors // 2, 2, wheel, local).transpose(1, 0, 3, 2)
    out = np.zeros((2, COMPS, sectors // 2, COMPS, local, wheel), np.float32)
    for c in range(COMPS):
        out[:, c, :, c] = table
    out = out.reshape(2 * COMPS * (sectors // 2), COMPS * sectors)
    high = out.astype(jnp.bfloat16)
    low = (out - high.astype(np.float32)).astype(jnp.bfloat16)
    return np.concatenate((low, high, high), axis=1)


def split(x):
    high = x.astype(BF)
    return high, (x - high.astype(F32)).astype(BF)


def dot(a, b):
    return jnp.dot(a, b, preferred_element_type=F32)


def rows_of(local):
    return 2 * local * COMPS, local * COMPS


def spot(places, slabs, device, side):
    if slabs == 2:
        return jnp.where(side == 0, places[2 * device], places[2 * device + 1])
    return 2 * places[device] + side


def pack_body(vecs, local, slabs, spread, places, krylov, blade, iface, faces, *refs):
    kept = (len(refs) - 8) // 2
    sources, out, pick, targets = refs[:kept], refs[kept], refs[kept + 1], refs[kept + 2 : 2 * kept + 2]
    rows, moved, classes, names, sides, sems = refs[-6:]
    both, one = rows_of(local)
    data = both * vecs
    half = one * vecs
    halves = rows.shape[0] // data
    moves = [
        pltpu.make_async_copy(
            krylov.at[:, pl.ds(h * LANES, LANES)], rows.at[pl.ds(h * data, data)], sems.at[h]
        )
        for h in range(halves)
    ]
    small = [
        pltpu.make_async_copy(source, target, sems.at[halves + i])
        for i, (source, target) in enumerate(((blade, classes), (iface, names), (faces, sides)))
    ]
    rest = [
        pltpu.make_async_copy(source, target, sems.at[halves + 3 + i])
        for i, (source, target) in enumerate(zip(sources, targets))
    ]
    for move in small + moves + rest:
        move.start()
    for move in small:
        move.wait()
    width = names.shape[1]
    index = lax.broadcasted_iota(jnp.int32, (pick.shape[0], width), 0)
    for i, side in enumerate((1, 0)):
        hit = index == sides[side : side + 1, :]
        pick[:, i * width : (i + 1) * width] = jnp.where(hit, 1.0, 0.0).astype(BF)
    moved[halves * half :, :] = jnp.zeros((moved.shape[0] - halves * half, LANES), F32)
    at = halves * half
    for l in range(local):
        scale = 1.0 + class_step * classes[l].astype(F32)
        moved[at : at + vecs, :] = jnp.full((vecs, LANES), scale, F32)
        at += vecs
    for side in range(2):
        moved[at : at + vecs, 0:width] = jnp.broadcast_to(
            names[side : side + 1, :].astype(F32), (vecs, width)
        )
        at += vecs
    for h, move in enumerate(moves):
        move.wait()
        u = rows[h * data : h * data + half, :]
        v = rows[h * data + half : (h + 1) * data, :]
        e = u + damping_ratio * v
        moved[h * half : (h + 1) * half, :] = e
        rows[h * data : h * data + half, :] = e
        rows[h * data + half : (h + 1) * data, :] = v - shift_value * u
    height = out.shape[1]
    mine = lax.axis_index("slab") if slabs == 2 else 0
    for v in range(vecs):
        for side, source in ((mine, rows), (1 - mine, moved)):
            chunk = source[pl.ds(v, height, stride=vecs), :].astype(BF)
            for i in range(spread):
                out[spot(places, slabs, v * spread + i, side)] = chunk
    for move in rest:
        move.wait()


def residual_body(slabs, wheel, local, width, places, leaving, x, *refs):
    ins, (out, rim, own, others, rows) = refs[:-5], refs[-5:]
    count = 1 if slabs == 2 else 2
    lows = ins[: 0 if slabs == 2 else count]
    pick, neighbors, stiffness, mass, table = ins[len(lows) :]
    nodes = neighbors.shape[1]
    halves = nodes // LANES
    sectors = wheel * local
    height = x.shape[1]
    slab = lax.axis_index("slab")
    both, one = rows_of(local)

    mine = slab if slabs == 2 else 0
    for w in range(wheel):
        at = slice(w * height, (w + 1) * height)
        own[at, :] = x[spot(places, slabs, w, mine)].astype(F32)
        others[0, at, :] = x[spot(places, slabs, w, 1 - mine)].astype(F32)
        for i, ref in enumerate(lows):
            others[1 + i, at, :] = ref[places[w]].astype(F32)
    first = 0 if slabs == 2 else 1

    def field(source, rows_half, start):
        return jnp.concatenate(
            [
                jnp.concatenate(
                    [
                        source[pl.ds(h * rows_half + start + l * COMPS + c, wheel, stride=height), :]
                        for h in range(halves)
                    ],
                    axis=1,
                )
                for c in range(COMPS)
                for l in range(local)
            ],
            axis=0,
        )

    moved, residual = field(own, both, 0), field(own, both, one)
    v = (residual + shift_value * moved) * (1.0 / (1.0 + shift_value * damping_ratio))
    moved = moved.astype(BF)
    extras = halves * one
    scale = jnp.concatenate(
        [others[0, pl.ds(extras + l, wheel, stride=height), :] for l in range(local)], axis=0
    )
    scale = jnp.concatenate([scale] * halves, axis=1)

    index = lax.broadcasted_iota(jnp.int32, (nodes, width), 0)
    for i in range(2):
        row = extras + local + 1 - i
        names = others[first + i % count, row : row + 1, 0:width].astype(jnp.int32)
        valid = (slab > 0) if i == 0 else (slab < slabs - 1)
        hit = (index == names) & valid
        rim[:, i * width : (i + 1) * width] = jnp.where(hit, 1.0, 0.0).astype(BF)
    rims = [
        dot(field(others.at[first + i], one, 0).astype(BF), rim[...]) for i in range(count)
    ]
    if count == 2:
        lane = lax.broadcasted_iota(jnp.int32, rims[0].shape, 1)
        rims = [jnp.where(lane < width, rims[0], rims[1])]

    faces = dot(moved, pick[...])
    turned = []
    lane = lax.broadcasted_iota(jnp.int32, (wheel, 2 * width), 1)
    for c in range(COMPS):
        parts = [
            faces[(c * local + l) * wheel : (c * local + l + 1) * wheel] for l in range(local)
        ]
        for l in range(local):
            before = parts[l - 1] if l else pltpu.roll(parts[-1], 1, axis=0)
            after = parts[l + 1] if l < local - 1 else pltpu.roll(parts[0], wheel - 1, axis=0)
            turned.append(jnp.where(lane < width, before, after))
    turned = jnp.concatenate(turned, axis=0)
    extended = jnp.concatenate((moved, rims[0].astype(BF), turned.astype(BF)), axis=1)

    kinds = 4 * COMPS
    pairs = sectors // 2
    block = COMPS * sectors

    def emit(t, *parts):
        harmonic = dot(table[:, : len(parts) * block], jnp.concatenate(parts, axis=0))
        for h in range(halves):
            for q in range(2):
                for c in range(COMPS):
                    at = (q * COMPS + c) * pairs
                    rows[
                        pl.ds(h * kinds + (q * 2 + t) * COMPS + c, pairs, stride=halves * kinds), :
                    ] = harmonic[at : at + pairs, h * LANES : (h + 1) * LANES]

    top = residual.astype(BF)
    emit(0, top, top)

    restore = [None] * COMPS
    index = lax.broadcasted_iota(jnp.int16, (extended.shape[1], nodes), 0)
    for k in range(neighbors.shape[0]):
        names = jnp.broadcast_to(neighbors[k : k + 1, :], (16, nodes)).astype(jnp.int16)
        hit = index == jnp.concatenate([names] * (extended.shape[1] // 16), axis=0)
        picked = dot(extended, jnp.where(hit, jnp.ones((), BF), jnp.zeros((), BF)))
        for d in range(COMPS):
            term = picked[d * sectors : (d + 1) * sectors]
            for c in range(COMPS):
                part = stiffness[c, d, k : k + 1, :] * term
                restore[c] = part if restore[c] is None else restore[c] + part

    vc = [v[c * sectors : (c + 1) * sectors] for c in range(COMPS)]
    lumped = [mass[c : c + 1, :] for c in range(COMPS)]
    gyro = (-(gyro_rate * lumped[0]) * vc[1], (gyro_rate * lumped[1]) * vc[0], None)
    residual = []
    for c in range(COMPS):
        part = -scale * restore[c] - (shift_value * lumped[c]) * vc[c]
        residual.append(part if gyro[c] is None else part - gyro[c])
    top, rest = split(jnp.concatenate(residual, axis=0))
    emit(1, top, top, rest)
    chunk = out.shape[1]
    for p in range(pairs):
        out[leaving[p]] = rows[p * chunk : (p + 1) * chunk, :].astype(BF)


def apply_body(vecs, spread, places, y, precond, out, rows, stage, sems):
    kinds = 4 * COMPS
    per = LANES // GROUP
    chunk = y.shape[1]
    halves = chunk // kinds
    for w, place in enumerate(places):
        rows[w * chunk : (w + 1) * chunk, :] = y[place].astype(F32)
    lane = lax.broadcasted_iota(jnp.int32, (vecs, LANES), 1)
    moves = []
    for h in range(halves):
        tiles = [[] for _ in range(per)]
        for j in range(kinds // per):
            blocks = [
                rows[pl.ds(h * kinds + j * per + r, vecs, stride=chunk * spread), :]
                for r in range(per)
            ]
            step = per // 2
            while step:
                shift = step * GROUP
                upper = (lane // shift) % 2 == 1
                fresh = list(blocks)
                for r in range(per):
                    if r & step == 0:
                        a, b = blocks[r], blocks[r + step]
                        fresh[r] = jnp.where(upper, pltpu.roll(b, shift, axis=1), a)
                        fresh[r + step] = jnp.where(
                            upper, b, pltpu.roll(a, LANES - shift, axis=1)
                        )
                blocks = fresh
                step //= 2
            for g in range(per):
                tiles[g].append(blocks[g].astype(BF))
        for g in range(per):
            lhs = jnp.concatenate(tiles[g], axis=1)
            at = h * per + g
            stage[at] = lax.dot_general(
                lhs,
                precond[at],
                (((1,), (1,)), ((), ())),
                preferred_element_type=F32,
            )
            moves.append(pltpu.make_async_copy(stage.at[at], out.at[at], sems.at[at]))
            moves[-1].start()
    for move in moves:
        move.wait()


def on_device(
    wheel, slabs, krylov_block, blade_class, neighbors, iface_rows, face_rows, stiffness, lumped_mass, precond
):
    states, local, comps, vecs, nodes = krylov_block.shape
    width = iface_rows.shape[1]
    spread = wheel // vecs
    sectors = wheel * local
    halves = nodes // LANES
    both, one = rows_of(local)
    height = halves * both
    vmem = pl.BlockSpec(memory_space=pltpu.VMEM)
    anywhere = pl.BlockSpec(memory_space=pl.ANY)
    places, devices = arrangement(wheel * slabs if slabs == 2 else wheel, FIRST)
    leaving, receivers = arrangement(wheel, SECOND)
    params = pltpu.CompilerParams(vmem_limit_bytes=LIMIT)

    kept = (neighbors, stiffness, lumped_mass, jnp.asarray(transform(wheel, local)))
    packed, *tables = pl.pallas_call(
        functools.partial(pack_body, vecs, local, slabs, spread, places),
        out_shape=(
            pltpu.VMEM((wheel * 2, height, LANES), BF),
            pltpu.VMEM((nodes, 2 * width), BF),
            *(pltpu.VMEM(x.shape, x.dtype) for x in kept),
        ),
        in_specs=[anywhere] * (4 + len(kept)),
        out_specs=(vmem,) * (2 + len(kept)),
        scratch_shapes=[
            pltpu.VMEM((height * vecs, LANES), F32),
            pltpu.VMEM((height * vecs, LANES), F32),
            pltpu.SMEM(blade_class.shape, jnp.int32),
            pltpu.VMEM(iface_rows.shape, jnp.int32),
            pltpu.VMEM(face_rows.shape, jnp.int32),
            pltpu.SemaphoreType.DMA((halves + 3 + len(kept),)),
        ],
        compiler_params=params,
        cost_estimate=pl.CostEstimate(flops=1000000000, bytes_accessed=10000000, transcendentals=0),
    )(
        hold(krylov_block.reshape(states * local * comps * vecs, nodes)),
        hold(blade_class),
        hold(iface_rows),
        hold(face_rows),
        *(hold(x) for x in kept),
    )
    if slabs == 2:
        got = lax.all_to_all(
            packed, ("wheel", "slab"), 0, 0, axis_index_groups=[devices], tiled=True
        )
        sides = ()
    else:
        got = lax.all_to_all(packed, "wheel", 0, 0, axis_index_groups=[devices], tiled=True)
        given = got[1::2]
        up = [(i, i + 1) for i in range(slabs - 1)]
        down = [(i + 1, i) for i in range(slabs - 1)]
        sides = (lax.ppermute(given, "slab", up), lax.ppermute(given, "slab", down))

    pairs = sectors // 2
    chunk = 4 * comps * halves
    sent = pl.pallas_call(
        functools.partial(residual_body, slabs, wheel, local, width, places, leaving),
        out_shape=pltpu.VMEM((pairs, chunk, LANES), BF),
        in_specs=[vmem] * (1 + len(sides) + len(tables)),
        out_specs=vmem,
        scratch_shapes=[
            pltpu.VMEM((nodes, 2 * width), BF),
            pltpu.VMEM((wheel * height, LANES), F32),
            pltpu.VMEM((1 + len(sides), wheel * height, LANES), F32),
            pltpu.VMEM((pairs * chunk, LANES), F32),
        ],
        compiler_params=params,
        cost_estimate=pl.CostEstimate(flops=1000000000, bytes_accessed=10000000, transcendentals=0),
    )(near(got), *(near(x) for x in sides), *(near(x) for x in tables))
    back = lax.all_to_all(sent, "wheel", 0, 0, axis_index_groups=[receivers], tiled=True)
    owned, groups, order, _ = precond.shape
    out = pl.pallas_call(
        functools.partial(apply_body, vecs, spread, leaving),
        out_shape=jax.ShapeDtypeStruct((groups, vecs, order), F32),
        in_specs=[vmem, vmem],
        out_specs=anywhere,
        scratch_shapes=[
            pltpu.VMEM((wheel * chunk, LANES), F32),
            pltpu.VMEM((groups, vecs, order), F32),
            pltpu.SemaphoreType.DMA((groups,)),
        ],
        compiler_params=params,
        cost_estimate=pl.CostEstimate(flops=1000000000, bytes_accessed=10000000, transcendentals=0),
    )(near(back), near(precond.reshape(groups, order, order)))
    return out.reshape(owned, groups, vecs, order)


def solution(mesh):
    return jax.shard_map(
        functools.partial(on_device, mesh.shape["wheel"], mesh.shape["slab"]),
        mesh=mesh,
        in_specs=(
            P(None, "wheel", None, None, "slab"),
            P("wheel"),
            P(None, "slab"),
            P(None, "slab"),
            P(None, "slab"),
            P(None, None, None, "slab"),
            P(None, "slab"),
            P("wheel", "slab", None, None),
        ),
        out_specs=P("wheel", "slab", None, None),
        check_vma=False,
    )
```

```python
import functools
import math

import jax
import jax.numpy as jnp
import numpy as np
from jax import lax
from jax.experimental import pallas as pl
from jax.experimental.pallas import tpu as pltpu
from jax.sharding import PartitionSpec as P

GROUP = 32
LANES = 128
COMPS = 3
LIMIT = 16 << 20

damping_ratio = 0.5
gyro_rate = 0.8
shift_value = 0.3
class_step = 0.125

BF = jnp.bfloat16
F32 = jnp.float32


FIRST = 165202023144815051924973138721503180
SECOND = 7663315406539


def arrangement(count, draw):
    left = list(range(count))
    devices = []
    while left:
        draw, pick = divmod(draw, len(left))
        devices.append(left.pop(pick))
    places = [0] * count
    for place, device in enumerate(devices):
        places[device] = place
    return places, devices


def hold(x):
    return pltpu.with_memory_space_constraint(x, pltpu.HBM)


def near(x):
    return pltpu.with_memory_space_constraint(x, pltpu.VMEM)


def basis(sectors_all):
    row = np.arange(sectors_all)[:, None]
    sector = np.arange(sectors_all)[None, :]
    pair, part = row // 2, row % 2
    angles = 2.0 * math.pi / sectors_all * (pair * sector % sectors_all)
    edge = np.where(part == 0, 1.0, 1.0 - 2.0 * (sector % 2)) * math.sqrt(1.0 / sectors_all)
    inner = np.where(part == 0, np.cos(angles), np.sin(angles)) * math.sqrt(2.0 / sectors_all)
    return np.where(pair == 0, edge, inner)


def transform(wheel, local):
    sectors = wheel * local
    table = basis(sectors).reshape(sectors // 2, 2, wheel, local).transpose(1, 0, 3, 2)
    out = np.zeros((2, COMPS, sectors // 2, COMPS, local, wheel), np.float32)
    for c in range(COMPS):
        out[:, c, :, c] = table
    out = out.reshape(2 * COMPS * (sectors // 2), COMPS * sectors)
    high = out.astype(jnp.bfloat16)
    low = (out - high.astype(np.float32)).astype(jnp.bfloat16)
    return np.concatenate((low, high, high), axis=1)


def split(x):
    high = x.astype(BF)
    return high, (x - high.astype(F32)).astype(BF)


def dot(a, b):
    return jnp.dot(a, b, preferred_element_type=F32)


def rows_of(local):
    return 2 * local * COMPS, local * COMPS


def spot(places, slabs, device, side):
    if slabs == 2:
        return jnp.where(side == 0, places[2 * device], places[2 * device + 1])
    return 2 * places[device] + side


def pack_body(vecs, local, slabs, spread, places, krylov, blade, iface, faces, *refs):
    kept = (len(refs) - 8) // 2
    sources, out, pick, targets = refs[:kept], refs[kept], refs[kept + 1], refs[kept + 2 : 2 * kept + 2]
    rows, moved, classes, names, sides, sems = refs[-6:]
    both, one = rows_of(local)
    data = both * vecs
    half = one * vecs
    halves = rows.shape[0] // data
    moves = [
        pltpu.make_async_copy(
            krylov.at[:, pl.ds(h * LANES, LANES)], rows.at[pl.ds(h * data, data)], sems.at[h]
        )
        for h in range(halves)
    ]
    small = [
        pltpu.make_async_copy(source, target, sems.at[halves + i])
        for i, (source, target) in enumerate(((blade, classes), (iface, names), (faces, sides)))
    ]
    rest = [
        pltpu.make_async_copy(source, target, sems.at[halves + 3 + i])
        for i, (source, target) in enumerate(zip(sources, targets))
    ]
    for move in small + moves + rest:
        move.start()
    for move in small:
        move.wait()
    width = names.shape[1]
    index = lax.broadcasted_iota(jnp.int32, (pick.shape[0], width), 0)
    for i, side in enumerate((1, 0)):
        hit = index == sides[side : side + 1, :]
        pick[:, i * width : (i + 1) * width] = jnp.where(hit, 1.0, 0.0).astype(BF)
    moved[halves * half :, :] = jnp.zeros((moved.shape[0] - halves * half, LANES), F32)
    at = halves * half
    for l in range(local):
        scale = 1.0 + class_step * classes[l].astype(F32)
        moved[at : at + vecs, :] = jnp.full((vecs, LANES), scale, F32)
        at += vecs
    for side in range(2):
        moved[at : at + vecs, 0:width] = jnp.broadcast_to(
            names[side : side + 1, :].astype(F32), (vecs, width)
        )
        at += vecs
    for h, move in enumerate(moves):
        move.wait()
        u = rows[h * data : h * data + half, :]
        v = rows[h * data + half : (h + 1) * data, :]
        e = u + damping_ratio * v
        moved[h * half : (h + 1) * half, :] = e
        rows[h * data : h * data + half, :] = e
        rows[h * data + half : (h + 1) * data, :] = v - shift_value * u
    height = out.shape[1]
    mine = lax.axis_index("slab") if slabs == 2 else 0
    for v in range(vecs):
        for side, source in ((mine, rows), (1 - mine, moved)):
            chunk = source[pl.ds(v, height, stride=vecs), :].astype(BF)
            for i in range(spread):
                out[spot(places, slabs, v * spread + i, side)] = chunk
    for move in rest:
        move.wait()


def residual_body(slabs, wheel, local, width, places, leaving, x, *refs):
    ins, (out, rim, own, others, rows) = refs[:-5], refs[-5:]
    count = 1 if slabs == 2 else 2
    lows = ins[: 0 if slabs == 2 else count]
    pick, neighbors, stiffness, mass, table = ins[len(lows) :]
    nodes = neighbors.shape[1]
    halves = nodes // LANES
    sectors = wheel * local
    height = x.shape[1]
    slab = lax.axis_index("slab")
    both, one = rows_of(local)

    mine = slab if slabs == 2 else 0
    for w in range(wheel):
        at = slice(w * height, (w + 1) * height)
        own[at, :] = x[spot(places, slabs, w, mine)].astype(F32)
        others[0, at, :] = x[spot(places, slabs, w, 1 - mine)].astype(F32)
        for i, ref in enumerate(lows):
            others[1 + i, at, :] = ref[places[w]].astype(F32)
    first = 0 if slabs == 2 else 1

    def field(source, rows_half, start):
        return jnp.concatenate(
            [
                jnp.concatenate(
                    [
                        source[pl.ds(h * rows_half + start + l * COMPS + c, wheel, stride=height), :]
                        for h in range(halves)
                    ],
                    axis=1,
                )
                for c in range(COMPS)
                for l in range(local)
            ],
            axis=0,
        )

    moved, residual = field(own, both, 0), field(own, both, one)
    v = (residual + shift_value * moved) * (1.0 / (1.0 + shift_value * damping_ratio))
    moved = moved.astype(BF)
    extras = halves * one
    scale = jnp.concatenate(
        [others[0, pl.ds(extras + l, wheel, stride=height), :] for l in range(local)], axis=0
    )
    scale = jnp.concatenate([scale] * halves, axis=1)

    index = lax.broadcasted_iota(jnp.int32, (nodes, width), 0)
    for i in range(2):
        row = extras + local + 1 - i
        names = others[first + i % count, row : row + 1, 0:width].astype(jnp.int32)
        valid = (slab > 0) if i == 0 else (slab < slabs - 1)
        hit = (index == names) & valid
        rim[:, i * width : (i + 1) * width] = jnp.where(hit, 1.0, 0.0).astype(BF)
    rims = [
        dot(field(others.at[first + i], one, 0).astype(BF), rim[...]) for i in range(count)
    ]
    if count == 2:
        lane = lax.broadcasted_iota(jnp.int32, rims[0].shape, 1)
        rims = [jnp.where(lane < width, rims[0], rims[1])]

    faces = dot(moved, pick[...])
    turned = []
    lane = lax.broadcasted_iota(jnp.int32, (wheel, 2 * width), 1)
    for c in range(COMPS):
        parts = [
            faces[(c * local + l) * wheel : (c * local + l + 1) * wheel] for l in range(local)
        ]
        for l in range(local):
            before = parts[l - 1] if l else pltpu.roll(parts[-1], 1, axis=0)
            after = parts[l + 1] if l < local - 1 else pltpu.roll(parts[0], wheel - 1, axis=0)
            turned.append(jnp.where(lane < width, before, after))
    turned = jnp.concatenate(turned, axis=0)
    extended = jnp.concatenate((moved, rims[0].astype(BF), turned.astype(BF)), axis=1)

    kinds = 4 * COMPS
    pairs = sectors // 2
    block = COMPS * sectors

    def emit(t, *parts):
        harmonic = dot(table[:, : len(parts) * block], jnp.concatenate(parts, axis=0))
        for h in range(halves):
            for q in range(2):
                for c in range(COMPS):
                    at = (q * COMPS + c) * pairs
                    rows[
                        pl.ds(h * kinds + (q * 2 + t) * COMPS + c, pairs, stride=halves * kinds), :
                    ] = harmonic[at : at + pairs, h * LANES : (h + 1) * LANES]

    top = residual.astype(BF)
    emit(0, top, top)

    restore = [None] * COMPS
    index = lax.broadcasted_iota(jnp.int16, (extended.shape[1], nodes), 0)
    for k in range(neighbors.shape[0]):
        names = jnp.broadcast_to(neighbors[k : k + 1, :], (16, nodes)).astype(jnp.int16)
        hit = index == jnp.concatenate([names] * (extended.shape[1] // 16), axis=0)
        picked = dot(extended, jnp.where(hit, jnp.ones((), BF), jnp.zeros((), BF)))
        for d in range(COMPS):
            term = picked[d * sectors : (d + 1) * sectors]
            for c in range(COMPS):
                part = stiffness[c, d, k : k + 1, :] * term
                restore[c] = part if restore[c] is None else restore[c] + part

    vc = [v[c * sectors : (c + 1) * sectors] for c in range(COMPS)]
    lumped = [mass[c : c + 1, :] for c in range(COMPS)]
    gyro = (-(gyro_rate * lumped[0]) * vc[1], (gyro_rate * lumped[1]) * vc[0], None)
    residual = []
    for c in range(COMPS):
        part = -scale * restore[c] - (shift_value * lumped[c]) * vc[c]
        residual.append(part if gyro[c] is None else part - gyro[c])
    top, rest = split(jnp.concatenate(residual, axis=0))
    emit(1, top, top, rest)
    chunk = out.shape[1]
    for p in range(pairs):
        out[leaving[p]] = rows[p * chunk : (p + 1) * chunk, :].astype(BF)


def apply_body(vecs, spread, places, y, precond, out, rows, stage, sems):
    kinds = 4 * COMPS
    per = LANES // GROUP
    chunk = y.shape[1]
    halves = chunk // kinds
    for w, place in enumerate(places):
        rows[w * chunk : (w + 1) * chunk, :] = y[place].astype(F32)
    lane = lax.broadcasted_iota(jnp.int32, (vecs, LANES), 1)
    moves = []
    for h in range(halves):
        tiles = [[] for _ in range(per)]
        for j in range(kinds // per):
            blocks = [
                rows[pl.ds(h * kinds + j * per + r, vecs, stride=chunk * spread), :]
                for r in range(per)
            ]
            step = per // 2
            while step:
                shift = step * GROUP
                upper = (lane // shift) % 2 == 1
                fresh = list(blocks)
                for r in range(per):
                    if r & step == 0:
                        a, b = blocks[r], blocks[r + step]
                        fresh[r] = jnp.where(upper, pltpu.roll(b, shift, axis=1), a)
                        fresh[r + step] = jnp.where(
                            upper, b, pltpu.roll(a, LANES - shift, axis=1)
                        )
                blocks = fresh
                step //= 2
            for g in range(per):
                tiles[g].append(blocks[g].astype(BF))
        for g in range(per):
            lhs = jnp.concatenate(tiles[g], axis=1)
            at = h * per + g
            stage[at] = lax.dot_general(
                lhs,
                precond[at],
                (((1,), (1,)), ((), ())),
                preferred_element_type=F32,
            )
            moves.append(pltpu.make_async_copy(stage.at[at], out.at[at], sems.at[at]))
            moves[-1].start()
    for move in moves:
        move.wait()


def on_device(
    wheel, slabs, krylov_block, blade_class, neighbors, iface_rows, face_rows, stiffness, lumped_mass, precond
):
    states, local, comps, vecs, nodes = krylov_block.shape
    width = iface_rows.shape[1]
    spread = wheel // vecs
    sectors = wheel * local
    halves = nodes // LANES
    both, one = rows_of(local)
    height = halves * both
    vmem = pl.BlockSpec(memory_space=pltpu.VMEM)
    anywhere = pl.BlockSpec(memory_space=pl.ANY)
    places, devices = arrangement(wheel * slabs if slabs == 2 else wheel, FIRST)
    leaving, receivers = arrangement(wheel, SECOND)
    params = pltpu.CompilerParams(vmem_limit_bytes=LIMIT)

    kept = (neighbors, stiffness, lumped_mass, jnp.asarray(transform(wheel, local)))
    packed, *tables = pl.pallas_call(
        functools.partial(pack_body, vecs, local, slabs, spread, places),
        out_shape=(
            pltpu.VMEM((wheel * 2, height, LANES), BF),
            pltpu.VMEM((nodes, 2 * width), BF),
            *(pltpu.VMEM(x.shape, x.dtype) for x in kept),
        ),
        in_specs=[anywhere] * (4 + len(kept)),
        out_specs=(vmem,) * (2 + len(kept)),
        scratch_shapes=[
            pltpu.VMEM((height * vecs, LANES), F32),
            pltpu.VMEM((height * vecs, LANES), F32),
            pltpu.SMEM(blade_class.shape, jnp.int32),
            pltpu.VMEM(iface_rows.shape, jnp.int32),
            pltpu.VMEM(face_rows.shape, jnp.int32),
            pltpu.SemaphoreType.DMA((halves + 3 + len(kept),)),
        ],
        compiler_params=params,
        cost_estimate=pl.CostEstimate(flops=1000000000, bytes_accessed=10000000, transcendentals=0),
    )(
        hold(krylov_block.reshape(states * local * comps * vecs, nodes)),
        hold(blade_class),
        hold(iface_rows),
        hold(face_rows),
        *(hold(x) for x in kept),
    )
    if slabs == 2:
        got = lax.all_to_all(
            packed, ("wheel", "slab"), 0, 0, axis_index_groups=[devices], tiled=True
        )
        sides = ()
    else:
        got = lax.all_to_all(packed, "wheel", 0, 0, axis_index_groups=[devices], tiled=True)
        given = got[1::2]
        up = [(i, i + 1) for i in range(slabs - 1)]
        down = [(i + 1, i) for i in range(slabs - 1)]
        sides = (lax.ppermute(given, "slab", up), lax.ppermute(given, "slab", down))

    pairs = sectors // 2
    chunk = 4 * comps * halves
    sent = pl.pallas_call(
        functools.partial(residual_body, slabs, wheel, local, width, places, leaving),
        out_shape=pltpu.VMEM((pairs, chunk, LANES), BF),
        in_specs=[vmem] * (1 + len(sides) + len(tables)),
        out_specs=vmem,
        scratch_shapes=[
            pltpu.VMEM((nodes, 2 * width), BF),
            pltpu.VMEM((wheel * height, LANES), F32),
            pltpu.VMEM((1 + len(sides), wheel * height, LANES), F32),
            pltpu.VMEM((pairs * chunk, LANES), F32),
        ],
        compiler_params=params,
        cost_estimate=pl.CostEstimate(flops=1000000000, bytes_accessed=10000000, transcendentals=0),
    )(near(got), *(near(x) for x in sides), *(near(x) for x in tables))
    back = lax.all_to_all(sent, "wheel", 0, 0, axis_index_groups=[receivers], tiled=True)
    owned, groups, order, _ = precond.shape
    out = pl.pallas_call(
        functools.partial(apply_body, vecs, spread, leaving),
        out_shape=jax.ShapeDtypeStruct((groups, vecs, order), F32),
        in_specs=[vmem, vmem],
        out_specs=anywhere,
        scratch_shapes=[
            pltpu.VMEM((wheel * chunk, LANES), F32),
            pltpu.VMEM((groups, vecs, order), F32),
            pltpu.SemaphoreType.DMA((groups,)),
        ],
        compiler_params=params,
        cost_estimate=pl.CostEstimate(flops=1000000000, bytes_accessed=10000000, transcendentals=0),
    )(near(back), near(precond.reshape(groups, order, order)))
    return out.reshape(owned, groups, vecs, order)


def solution(mesh):
    return jax.shard_map(
        functools.partial(on_device, mesh.shape["wheel"], mesh.shape["slab"]),
        mesh=mesh,
        in_specs=(
            P(None, "wheel", None, None, "slab"),
            P("wheel"),
            P(None, "slab"),
            P(None, "slab"),
            P(None, "slab"),
            P(None, None, None, "slab"),
            P(None, "slab"),
            P("wheel", "slab", None, None),
        ),
        out_specs=P("wheel", "slab", None, None),
        check_vma=False,
    )
```

```python
import functools
import math

import jax
import jax.numpy as jnp
import numpy as np
from jax import lax
from jax.experimental import pallas as pl
from jax.experimental.pallas import tpu as pltpu
from jax.sharding import PartitionSpec as P

GROUP = 32
LANES = 128
COMPS = 3
LIMIT = 16 << 20

damping_ratio = 0.5
gyro_rate = 0.8
shift_value = 0.3
class_step = 0.125

BF = jnp.bfloat16
F32 = jnp.float32


FIRST = 165202023144815051924973138721503180
SECOND = 7663315406539


def arrangement(count, draw):
    left = list(range(count))
    devices = []
    while left:
        draw, pick = divmod(draw, len(left))
        devices.append(left.pop(pick))
    places = [0] * count
    for place, device in enumerate(devices):
        places[device] = place
    return places, devices


def hold(x):
    return pltpu.with_memory_space_constraint(x, pltpu.HBM)


def near(x):
    return pltpu.with_memory_space_constraint(x, pltpu.VMEM)


def basis(sectors_all):
    row = np.arange(sectors_all)[:, None]
    sector = np.arange(sectors_all)[None, :]
    pair, part = row // 2, row % 2
    angles = 2.0 * math.pi / sectors_all * (pair * sector % sectors_all)
    edge = np.where(part == 0, 1.0, 1.0 - 2.0 * (sector % 2)) * math.sqrt(1.0 / sectors_all)
    inner = np.where(part == 0, np.cos(angles), np.sin(angles)) * math.sqrt(2.0 / sectors_all)
    return np.where(pair == 0, edge, inner)


def transform(wheel, local):
    sectors = wheel * local
    table = basis(sectors).reshape(sectors // 2, 2, wheel, local).transpose(1, 0, 3, 2)
    out = np.zeros((2, COMPS, sectors // 2, COMPS, local, wheel), np.float32)
    for c in range(COMPS):
        out[:, c, :, c] = table
    out = out.reshape(2 * COMPS * (sectors // 2), COMPS * sectors)
    high = out.astype(jnp.bfloat16)
    low = (out - high.astype(np.float32)).astype(jnp.bfloat16)
    return np.concatenate((low, high, high), axis=1)


def split(x):
    high = x.astype(BF)
    return high, (x - high.astype(F32)).astype(BF)


def dot(a, b):
    return jnp.dot(a, b, preferred_element_type=F32)


def rows_of(local):
    return 2 * local * COMPS, local * COMPS


def spot(places, slabs, device, side):
    if slabs == 2:
        return jnp.where(side == 0, places[2 * device], places[2 * device + 1])
    return 2 * places[device] + side


def pack_body(vecs, local, slabs, spread, places, krylov, blade, iface, faces, *refs):
    kept = (len(refs) - 8) // 2
    sources, out, pick, targets = refs[:kept], refs[kept], refs[kept + 1], refs[kept + 2 : 2 * kept + 2]
    rows, moved, classes, names, sides, sems = refs[-6:]
    both, one = rows_of(local)
    data = both * vecs
    half = one * vecs
    halves = rows.shape[0] // data
    moves = [
        pltpu.make_async_copy(
            krylov.at[:, pl.ds(h * LANES, LANES)], rows.at[pl.ds(h * data, data)], sems.at[h]
        )
        for h in range(halves)
    ]
    small = [
        pltpu.make_async_copy(source, target, sems.at[halves + i])
        for i, (source, target) in enumerate(((blade, classes), (iface, names), (faces, sides)))
    ]
    rest = [
        pltpu.make_async_copy(source, target, sems.at[halves + 3 + i])
        for i, (source, target) in enumerate(zip(sources, targets))
    ]
    for move in small + moves + rest:
        move.start()
    for move in small:
        move.wait()
    width = names.shape[1]
    index = lax.broadcasted_iota(jnp.int32, (pick.shape[0], width), 0)
    for i, side in enumerate((1, 0)):
        hit = index == sides[side : side + 1, :]
        pick[:, i * width : (i + 1) * width] = jnp.where(hit, 1.0, 0.0).astype(BF)
    moved[halves * half :, :] = jnp.zeros((moved.shape[0] - halves * half, LANES), F32)
    at = halves * half
    for l in range(local):
        scale = 1.0 + class_step * classes[l].astype(F32)
        moved[at : at + vecs, :] = jnp.full((vecs, LANES), scale, F32)
        at += vecs
    for side in range(2):
        moved[at : at + vecs, 0:width] = jnp.broadcast_to(
            names[side : side + 1, :].astype(F32), (vecs, width)
        )
        at += vecs
    for h, move in enumerate(moves):
        move.wait()
        u = rows[h * data : h * data + half, :]
        v = rows[h * data + half : (h + 1) * data, :]
        e = u + damping_ratio * v
        moved[h * half : (h + 1) * half, :] = e
        rows[h * data : h * data + half, :] = e
        rows[h * data + half : (h + 1) * data, :] = v - shift_value * u
    height = out.shape[1]
    mine = lax.axis_index("slab") if slabs == 2 else 0
    for v in range(vecs):
        for side, source in ((mine, rows), (1 - mine, moved)):
            chunk = source[pl.ds(v, height, stride=vecs), :].astype(BF)
            for i in range(spread):
                out[spot(places, slabs, v * spread + i, side)] = chunk
    for move in rest:
        move.wait()


def residual_body(slabs, wheel, local, width, places, leaving, x, *refs):
    ins, (out, rim, own, others, rows) = refs[:-5], refs[-5:]
    count = 1 if slabs == 2 else 2
    lows = ins[: 0 if slabs == 2 else count]
    pick, neighbors, stiffness, mass, table = ins[len(lows) :]
    nodes = neighbors.shape[1]
    halves = nodes // LANES
    sectors = wheel * local
    height = x.shape[1]
    slab = lax.axis_index("slab")
    both, one = rows_of(local)

    mine = slab if slabs == 2 else 0
    for w in range(wheel):
        at = slice(w * height, (w + 1) * height)
        own[at, :] = x[spot(places, slabs, w, mine)].astype(F32)
        others[0, at, :] = x[spot(places, slabs, w, 1 - mine)].astype(F32)
        for i, ref in enumerate(lows):
            others[1 + i, at, :] = ref[places[w]].astype(F32)
    first = 0 if slabs == 2 else 1

    def field(source, rows_half, start):
        return jnp.concatenate(
            [
                jnp.concatenate(
                    [
                        source[pl.ds(h * rows_half + start + l * COMPS + c, wheel, stride=height), :]
                        for h in range(halves)
                    ],
                    axis=1,
                )
                for c in range(COMPS)
                for l in range(local)
            ],
            axis=0,
        )

    moved, residual = field(own, both, 0), field(own, both, one)
    v = (residual + shift_value * moved) * (1.0 / (1.0 + shift_value * damping_ratio))
    moved = moved.astype(BF)
    extras = halves * one
    scale = jnp.concatenate(
        [others[0, pl.ds(extras + l, wheel, stride=height), :] for l in range(local)], axis=0
    )
    scale = jnp.concatenate([scale] * halves, axis=1)

    index = lax.broadcasted_iota(jnp.int32, (nodes, width), 0)
    for i in range(2):
        row = extras + local + 1 - i
        names = others[first + i % count, row : row + 1, 0:width].astype(jnp.int32)
        valid = (slab > 0) if i == 0 else (slab < slabs - 1)
        hit = (index == names) & valid
        rim[:, i * width : (i + 1) * width] = jnp.where(hit, 1.0, 0.0).astype(BF)
    rims = [
        dot(field(others.at[first + i], one, 0).astype(BF), rim[...]) for i in range(count)
    ]
    if count == 2:
        lane = lax.broadcasted_iota(jnp.int32, rims[0].shape, 1)
        rims = [jnp.where(lane < width, rims[0], rims[1])]

    faces = dot(moved, pick[...])
    turned = []
    lane = lax.broadcasted_iota(jnp.int32, (wheel, 2 * width), 1)
    for c in range(COMPS):
        parts = [
            faces[(c * local + l) * wheel : (c * local + l + 1) * wheel] for l in range(local)
        ]
        for l in range(local):
            before = parts[l - 1] if l else pltpu.roll(parts[-1], 1, axis=0)
            after = parts[l + 1] if l < local - 1 else pltpu.roll(parts[0], wheel - 1, axis=0)
            turned.append(jnp.where(lane < width, before, after))
    turned = jnp.concatenate(turned, axis=0)
    extended = jnp.concatenate((moved, rims[0].astype(BF), turned.astype(BF)), axis=1)

    kinds = 4 * COMPS
    pairs = sectors // 2
    block = COMPS * sectors

    def emit(t, *parts):
        harmonic = dot(table[:, : len(parts) * block], jnp.concatenate(parts, axis=0))
        for h in range(halves):
            for q in range(2):
                for c in range(COMPS):
                    at = (q * COMPS + c) * pairs
                    rows[
                        pl.ds(h * kinds + (q * 2 + t) * COMPS + c, pairs, stride=halves * kinds), :
                    ] = harmonic[at : at + pairs, h * LANES : (h + 1) * LANES]

    top = residual.astype(BF)
    emit(0, top, top)

    restore = [None] * COMPS
    index = lax.broadcasted_iota(jnp.int16, (extended.shape[1], nodes), 0)
    for k in range(neighbors.shape[0]):
        names = jnp.broadcast_to(neighbors[k : k + 1, :], (16, nodes)).astype(jnp.int16)
        hit = index == jnp.concatenate([names] * (extended.shape[1] // 16), axis=0)
        picked = dot(extended, jnp.where(hit, jnp.ones((), BF), jnp.zeros((), BF)))
        for d in range(COMPS):
            term = picked[d * sectors : (d + 1) * sectors]
            for c in range(COMPS):
                part = stiffness[c, d, k : k + 1, :] * term
                restore[c] = part if restore[c] is None else restore[c] + part

    vc = [v[c * sectors : (c + 1) * sectors] for c in range(COMPS)]
    lumped = [mass[c : c + 1, :] for c in range(COMPS)]
    gyro = (-(gyro_rate * lumped[0]) * vc[1], (gyro_rate * lumped[1]) * vc[0], None)
    residual = []
    for c in range(COMPS):
        part = -scale * restore[c] - (shift_value * lumped[c]) * vc[c]
        residual.append(part if gyro[c] is None else part - gyro[c])
    top, rest = split(jnp.concatenate(residual, axis=0))
    emit(1, top, top, rest)
    chunk = out.shape[1]
    for p in range(pairs):
        out[leaving[p]] = rows[p * chunk : (p + 1) * chunk, :].astype(BF)


def apply_body(vecs, spread, places, y, precond, out, rows, stage, sems):
    kinds = 4 * COMPS
    per = LANES // GROUP
    chunk = y.shape[1]
    halves = chunk // kinds
    for w, place in enumerate(places):
        rows[w * chunk : (w + 1) * chunk, :] = y[place].astype(F32)
    lane = lax.broadcasted_iota(jnp.int32, (vecs, LANES), 1)
    moves = []
    for h in range(halves):
        tiles = [[] for _ in range(per)]
        for j in range(kinds // per):
            blocks = [
                rows[pl.ds(h * kinds + j * per + r, vecs, stride=chunk * spread), :]
                for r in range(per)
            ]
            step = per // 2
            while step:
                shift = step * GROUP
                upper = (lane // shift) % 2 == 1
                fresh = list(blocks)
                for r in range(per):
                    if r & step == 0:
                        a, b = blocks[r], blocks[r + step]
                        fresh[r] = jnp.where(upper, pltpu.roll(b, shift, axis=1), a)
                        fresh[r + step] = jnp.where(
                            upper, b, pltpu.roll(a, LANES - shift, axis=1)
                        )
                blocks = fresh
                step //= 2
            for g in range(per):
                tiles[g].append(blocks[g].astype(BF))
        for g in range(per):
            lhs = jnp.concatenate(tiles[g], axis=1)
            at = h * per + g
            stage[at] = lax.dot_general(
                lhs,
                precond[at],
                (((1,), (1,)), ((), ())),
                preferred_element_type=F32,
            )
            moves.append(pltpu.make_async_copy(stage.at[at], out.at[at], sems.at[at]))
            moves[-1].start()
    for move in moves:
        move.wait()


def on_device(
    wheel, slabs, krylov_block, blade_class, neighbors, iface_rows, face_rows, stiffness, lumped_mass, precond
):
    states, local, comps, vecs, nodes = krylov_block.shape
    width = iface_rows.shape[1]
    spread = wheel // vecs
    sectors = wheel * local
    halves = nodes // LANES
    both, one = rows_of(local)
    height = halves * both
    vmem = pl.BlockSpec(memory_space=pltpu.VMEM)
    anywhere = pl.BlockSpec(memory_space=pl.ANY)
    places, devices = arrangement(wheel * slabs if slabs == 2 else wheel, FIRST)
    leaving, receivers = arrangement(wheel, SECOND)
    params = pltpu.CompilerParams(vmem_limit_bytes=LIMIT)

    kept = (neighbors, stiffness, lumped_mass, jnp.asarray(transform(wheel, local)))
    packed, *tables = pl.pallas_call(
        functools.partial(pack_body, vecs, local, slabs, spread, places),
        out_shape=(
            pltpu.VMEM((wheel * 2, height, LANES), BF),
            pltpu.VMEM((nodes, 2 * width), BF),
            *(pltpu.VMEM(x.shape, x.dtype) for x in kept),
        ),
        in_specs=[anywhere] * (4 + len(kept)),
        out_specs=(vmem,) * (2 + len(kept)),
        scratch_shapes=[
            pltpu.VMEM((height * vecs, LANES), F32),
            pltpu.VMEM((height * vecs, LANES), F32),
            pltpu.SMEM(blade_class.shape, jnp.int32),
            pltpu.VMEM(iface_rows.shape, jnp.int32),
            pltpu.VMEM(face_rows.shape, jnp.int32),
            pltpu.SemaphoreType.DMA((halves + 3 + len(kept),)),
        ],
        compiler_params=params,
        cost_estimate=pl.CostEstimate(flops=10000000000, bytes_accessed=100000000, transcendentals=0),
    )(
        hold(krylov_block.reshape(states * local * comps * vecs, nodes)),
        hold(blade_class),
        hold(iface_rows),
        hold(face_rows),
        *(hold(x) for x in kept),
    )
    if slabs == 2:
        got = lax.all_to_all(
            packed, ("wheel", "slab"), 0, 0, axis_index_groups=[devices], tiled=True
        )
        sides = ()
    else:
        got = lax.all_to_all(packed, "wheel", 0, 0, axis_index_groups=[devices], tiled=True)
        given = got[1::2]
        up = [(i, i + 1) for i in range(slabs - 1)]
        down = [(i + 1, i) for i in range(slabs - 1)]
        sides = (lax.ppermute(given, "slab", up), lax.ppermute(given, "slab", down))

    pairs = sectors // 2
    chunk = 4 * comps * halves
    sent = pl.pallas_call(
        functools.partial(residual_body, slabs, wheel, local, width, places, leaving),
        out_shape=pltpu.VMEM((pairs, chunk, LANES), BF),
        in_specs=[vmem] * (1 + len(sides) + len(tables)),
        out_specs=vmem,
        scratch_shapes=[
            pltpu.VMEM((nodes, 2 * width), BF),
            pltpu.VMEM((wheel * height, LANES), F32),
            pltpu.VMEM((1 + len(sides), wheel * height, LANES), F32),
            pltpu.VMEM((pairs * chunk, LANES), F32),
        ],
        compiler_params=params,
        cost_estimate=pl.CostEstimate(flops=10000000000, bytes_accessed=100000000, transcendentals=0),
    )(near(got), *(near(x) for x in sides), *(near(x) for x in tables))
    back = lax.all_to_all(sent, "wheel", 0, 0, axis_index_groups=[receivers], tiled=True)
    owned, groups, order, _ = precond.shape
    out = pl.pallas_call(
        functools.partial(apply_body, vecs, spread, leaving),
        out_shape=jax.ShapeDtypeStruct((groups, vecs, order), F32),
        in_specs=[vmem, vmem],
        out_specs=anywhere,
        scratch_shapes=[
            pltpu.VMEM((wheel * chunk, LANES), F32),
            pltpu.VMEM((groups, vecs, order), F32),
            pltpu.SemaphoreType.DMA((groups,)),
        ],
        compiler_params=params,
        cost_estimate=pl.CostEstimate(flops=10000000000, bytes_accessed=100000000, transcendentals=0),
    )(near(back), near(precond.reshape(groups, order, order)))
    return out.reshape(owned, groups, vecs, order)


def solution(mesh):
    return jax.shard_map(
        functools.partial(on_device, mesh.shape["wheel"], mesh.shape["slab"]),
        mesh=mesh,
        in_specs=(
            P(None, "wheel", None, None, "slab"),
            P("wheel"),
            P(None, "slab"),
            P(None, "slab"),
            P(None, "slab"),
            P(None, None, None, "slab"),
            P(None, "slab"),
            P("wheel", "slab", None, None),
        ),
        out_specs=P("wheel", "slab", None, None),
        check_vma=False,
    )
```
